32 devices in a mesh: group: 2 (over x), dp: 8 (over z, y), section: 2 (over core).
Axes of the slice: x: 2, y: 2, z: 4, core: 2. Of those that a mesh axis runs over, the one named last changes fastest.
Arguments:
- queries: bfloat16 [6144, 2048], P(('group', 'dp'), 'section'), parts along dimension 0, may hold values from -3 to 3
- grad_out: bfloat16 [6144, 2048], P(('group', 'dp'), 'section'), parts along dimension 0, may hold values from -16 to 16
- log_sums: float32 [16, 6144], P('section', ('group', 'dp')), parts along dimension 1, may hold values from 5 to 7
- neighbours: bfloat16 [96, 256, 896], P(('group', 'dp')), parts along dimension 0, may hold values from -3 to 3
- key_weight: bfloat16 [896, 2048], P(None, 'section'), may hold values from -0.1875 to 0.1875
- value_weight: bfloat16 [896, 2048], P(None, 'section'), may hold values from -0.1875 to 0.1875
- neighbour_ids: int32 [96, 2], P(('group', 'dp')), parts along dimension 0, may hold values from 0 to 31, as said below
- block_slot: int32 [64], P('group'), parts along dimension 0, may hold values from 0 to 31, as said below
- enc_input: bfloat16 [8192, 896], P(('group', 'dp')), parts along dimension 0, may hold values from -4 to 4
Outputs:
- query_grad: bfloat16 [6144, 2048], P(('group', 'dp'), 'section'), parts along dimension 0
- weight_grad: float32 [1792, 896], P(('group', 'dp', 'section')), parts along dimension 0
The draws below stay inside these ranges and needn't reach their ends.
There are 2 independent parts, one for each index of `group`. The reference program is written for one: setup_inputs(seed, part) draws one part's arguments, and reference() takes and returns one part's arrays. A program takes and returns all parts, laid end to end along the dimension named above; an argument that names none is the same for every part. Nothing has to cross between parts.
Inputs may be any that keep to these rules, and one draw needn't show every extreme that they name: `neighbour_ids`: the two entries of a span differ. With owner(n) = block_slot[n] // 4, among the 12 entries of the spans on one index of dp at most 3 have the same owner, and in every draw one owner gets exactly 3 from the spans of every index of dp. A permutation: block n is stored at block position block_slot[n] of enc_input.
All inputs are finite; a program needn't handle non-finite values.
Results may differ from the reference program's by a relative error of at most 0.006.
The reference program's roundings to bfloat16 on the way count: a program that leaves them out, or rounds other values in their place, can miss the bound.
Values may be sent and summed in bfloat16 or wider, within the bound.
No kernel may reach another device: no remote copies, remote signals or barrier semaphores. Data moves between devices by JAX's collectives and lax.ppermute only.
A program may use at most 128 MiB of HBM per device.

```python
from functools import partial
import jax
import jax.numpy as jnp
from jax import lax

H = 16
HD = 128
DE = 896
CL = 64
R = 128
CH_DEV = 6
NB_DEV = 4
SPANS = 48
TOKENS = 3072
NB = 32
CAP = 3


def neighbour_layout(key):
    base_key = jax.random.fold_in(key, 7)
    owner_count = NB // NB_DEV
    per_device = 2 * CH_DEV
    special = jax.random.randint(jax.random.fold_in(base_key, 1), (), 0, owner_count).astype(jnp.int32)
    others = ((special + 1 + jnp.arange(owner_count - 1)) % owner_count).astype(jnp.int32)
    owner_pool = jnp.repeat(others, CAP)

    def one_device(device_key):
        chosen = jax.random.permutation(jax.random.fold_in(device_key, 1), owner_pool)[:per_device - CAP]
        owners = jnp.concatenate([jnp.full((CAP,), special, dtype=jnp.int32), chosen.astype(jnp.int32)])
        owners = jax.random.permutation(jax.random.fold_in(device_key, 2), owners)
        first_idx = jax.random.randint(jax.random.fold_in(device_key, 3), (CH_DEV,), 0, NB_DEV)
        offset = jax.random.randint(jax.random.fold_in(device_key, 4), (CH_DEV,), 1, NB_DEV)
        second = (first_idx + offset) % NB_DEV
        local_idx = jnp.stack([first_idx, second], axis=1).reshape(per_device)
        return (owners * NB_DEV + local_idx).astype(jnp.int32)
    device_keys = jax.random.split(jax.random.fold_in(base_key, 2), owner_count)
    storage = jax.vmap(one_device)(device_keys).reshape(owner_count * CH_DEV, 2)
    shuffled = jax.random.permutation(jax.random.fold_in(base_key, 3), NB).astype(jnp.int32)
    inverse = jnp.argsort(shuffled).astype(jnp.int32)
    return (inverse[storage].astype(jnp.int32), shuffled)


def draw_neighbour_ids(key, part):
    return neighbour_layout(key)[0]


def draw_block_slot(key, part):
    return neighbour_layout(key)[1]


def spiked(result, own_key, source, target, shards_of, factor):
    def block_of(dim):
        return (jnp.arange(result.shape[dim]) // (result.shape[dim] // shards_of)).reshape((-1,) + (1,) * (result.ndim - 1 - dim))

    near = jax.random.permutation(own_key, shards_of)[block_of(target)]
    far = (block_of(target) + shards_of // 2) % shards_of
    return jnp.where((block_of(source) == near) | (block_of(source) == far), factor * result, result)


def block_levels(key, extent, pieces, low, largest):
    def one(position, blocks):
        steps = jax.random.uniform(jax.random.fold_in(jax.random.fold_in(key, 6), position), (blocks,), jnp.float32, low / len(pieces), largest / len(pieces))
        return jnp.repeat(jnp.exp(steps), extent[position] // blocks).reshape((-1,) + (1,) * (len(extent) - position - 1))

    gain = one(*pieces[0])
    for cut in pieces[1:]:
        gain = gain * one(*cut)
    return gain


def bell_draw(key, extent, deviation, reach, pieces=(), held_as=jnp.bfloat16):
    result = jax.random.normal(key, extent, jnp.float32) * deviation
    if len(pieces) > 0:
        result = block_levels(key, extent, pieces, -0.22, 0.18) * result
    return jnp.clip(result, min=-reach, max=reach).astype(held_as)


def noise_with(own_key, shape, deviation, limit, shards, heavy, kind=jnp.bfloat16):
    drawn = deviation * jax.random.normal(own_key, shape, jnp.float32)
    if shards:
        drawn = drawn * block_levels(own_key, shape, shards, -0.22, 0.18)
    return jnp.clip(spiked(drawn, jax.random.fold_in(own_key, 3), *heavy), -limit, limit).astype(kind)


def setup_inputs(seed: int = 0, part: int = 0) -> dict:
    arg_keys = jax.random.split(jax.random.key(seed), 10)
    part_splits = jax.random.split(jax.random.fold_in(arg_keys[9], part), 10)
    queries = bell_draw(part_splits[0], (TOKENS, H * HD), 1.0, 3.0, ((0, 8), (1, 2)))
    grad_out = bell_draw(part_splits[1], (TOKENS, H * HD), 4.0, 16.0, ((0, 8), (1, 2)))
    log_sums = jnp.clip(5.0 + 2.0 * jax.random.uniform(part_splits[2], (H, TOKENS), jnp.float32) ** block_levels(part_splits[2], (H, TOKENS), ((0, 2), (1, 8)), -0.2, 0.2), 5.0, 7.0)
    neighbours = bell_draw(part_splits[3], (SPANS, 2 * R, DE), 1.0, 3.0, ((0, 8),))
    key_weight = bell_draw(arg_keys[4], (DE, H * HD), DE ** -0.5, 0.1875, ((1, 2),))
    value_weight = bell_draw(arg_keys[5], (DE, H * HD), DE ** -0.5, 0.1875, ((1, 2),))
    neighbour_ids = draw_neighbour_ids(jax.random.fold_in(jax.random.fold_in(arg_keys[9], part), 71), part)
    block_slot = draw_block_slot(jax.random.fold_in(jax.random.fold_in(arg_keys[9], part), 71), part)
    enc_input = noise_with(part_splits[8], (NB * R, DE), 1.0, 4.0, ((0, 8),), (0, 1, 8, 2.0))
    return {"queries": queries, "grad_out": grad_out, "log_sums": log_sums, "neighbours": neighbours, "key_weight": key_weight, "value_weight": value_weight, "neighbour_ids": neighbour_ids, "block_slot": block_slot, "enc_input": enc_input}


def span_backward(key_weight, value_weight, items):
    queries, grad_out, log_sums, neighbours = items
    inv_root = HD ** -0.5
    key_rows = jnp.dot(neighbours, key_weight, preferred_element_type=jnp.float32).astype(jnp.bfloat16)
    value_rows = jnp.dot(neighbours, value_weight, preferred_element_type=jnp.float32).astype(jnp.bfloat16)
    query_heads = queries.astype(jnp.float32).reshape(CL, H, HD)
    grad_heads = grad_out.astype(jnp.float32).reshape(CL, H, HD)
    key_heads = key_rows.astype(jnp.float32).reshape(2 * R, H, HD)
    value_heads = value_rows.astype(jnp.float32).reshape(2 * R, H, HD)
    scores = jnp.einsum('qhe,khe->hqk', query_heads, key_heads) * inv_root
    prob_rows = jnp.exp(scores - log_sums[:, :, None])
    prob_grad = jnp.einsum('qhe,khe->hqk', grad_heads, value_heads)
    row_delta = jnp.sum(prob_rows * prob_grad, axis=2, keepdims=True)
    score_grad = prob_rows * (prob_grad - row_delta)
    prob_bf = lax.optimization_barrier(prob_rows.astype(jnp.bfloat16)).astype(jnp.float32)
    score_bf = lax.optimization_barrier(score_grad.astype(jnp.bfloat16)).astype(jnp.float32)
    query_grad = (jnp.einsum('hqk,khe->qhe', score_bf, key_heads) * inv_root).astype(jnp.bfloat16)
    key_grad = (jnp.einsum('hqk,qhe->khe', score_bf, query_heads) * inv_root).astype(jnp.bfloat16)
    value_grad = jnp.einsum('hqk,qhe->khe', prob_bf, grad_heads).astype(jnp.bfloat16)
    key_grad = key_grad.reshape(2 * R, H * HD)
    value_grad = value_grad.reshape(2 * R, H * HD)
    half_cols = (H // 2) * HD
    total = jnp.zeros((2 * R, DE), jnp.float32)
    for half in range(2):
        lower = half * half_cols
        upper = lower + half_cols
        part_sum = jnp.dot(key_grad[:, lower:upper], key_weight[:, lower:upper].T, preferred_element_type=jnp.float32)
        part_sum = part_sum + jnp.dot(value_grad[:, lower:upper], value_weight[:, lower:upper].T, preferred_element_type=jnp.float32)
        total = total + lax.optimization_barrier(part_sum.astype(jnp.bfloat16)).astype(jnp.float32)
    return query_grad.reshape(CL, H * HD), total.astype(jnp.bfloat16)


def reference(queries, grad_out, log_sums, neighbours, key_weight, value_weight, neighbour_ids, block_slot, enc_input):
    query_blocks = queries.reshape(SPANS, CL, H * HD)
    grad_blocks = grad_out.reshape(SPANS, CL, H * HD)
    sum_blocks = log_sums.reshape(H, SPANS, CL).transpose(1, 0, 2)
    query_grad, ref_grad = lax.map(partial(span_backward, key_weight, value_weight), (query_blocks, grad_blocks, sum_blocks, neighbours))
    storage = block_slot[neighbour_ids.reshape(SPANS * 2).astype(jnp.int32)].astype(jnp.int32)
    ref_rows = ref_grad.reshape(SPANS * 2, R, DE).astype(jnp.float32)
    enc_total = jnp.zeros((NB, R, DE), jnp.float32).at[storage].add(ref_rows)
    enc_grad = enc_total.astype(jnp.bfloat16).reshape(NB * R, DE)
    weight_grad = jnp.dot(enc_input.T, enc_grad, preferred_element_type=jnp.float32) * ((NB * R) ** -0.5)
    return query_grad.reshape(TOKENS, H * HD), weight_grad
```

```python
import functools

import jax
import jax.numpy as jnp
from jax import lax
from jax.experimental import pallas as pl
from jax.experimental.pallas import tpu as pltpu
from jax.sharding import PartitionSpec as P

HD = 128
DE = 896
CL = 64
R = 128
HR = R // 2
STEP = 2
CHUNKS = (1, 2)
F32 = jnp.float32
BF16 = jnp.bfloat16
NT = (((1,), (1,)), ((), ()))
TN = (((0,), (0,)), ((), ()))


def _dot(a, b, dims=(((1,), (0,)), ((), ()))):
    return lax.dot_general(a, b, dims, preferred_element_type=F32)


def _span_kernel(sec_ref, q_ref, g_ref, l_ref, n_ref, wk_ref, wv_ref, *rest):
    dq_ref, mine_ref, send_ref = rest[-3:]
    sec = sec_ref[0]
    near = pl.multiple_of(sec * HR, HR)
    far = pl.multiple_of((1 - sec) * HR, HR)
    inv_root = HD ** (-0.5)
    pieces = []
    for a in range(STEP):
        for base in (near, far):
            for k in range(2):
                pieces.append(n_ref[a, pl.ds(base + k * R, HR), :])
    rows = jnp.concatenate(pieces, axis=0)
    keys = _dot(rows, wk_ref[...]).astype(BF16)
    values = _dot(rows, wv_ref[...]).astype(BF16)
    pairs = q_ref.shape[1] // (2 * HD)
    left = lax.broadcasted_iota(jnp.int32, (CL, 2 * HD), 1) < HD
    low = lax.broadcasted_iota(jnp.int32, (1, 2 * CL), 1) < CL
    key_parts, value_parts = [], []
    for a in range(STEP):
        key_cols, value_cols = [], []
        for p in range(pairs):
            cols = slice(2 * HD * p, 2 * HD * (p + 1))
            ks = keys[2 * R * a : 2 * R * (a + 1), cols]
            vs = values[2 * R * a : 2 * R * (a + 1), cols]
            q = q_ref[CL * a : CL * (a + 1), cols]
            g = g_ref[CL * a : CL * (a + 1), cols]
            zero = jnp.zeros_like(q)
            qd = jnp.concatenate([jnp.where(left, q, zero), jnp.where(left, zero, q)], axis=0)
            gd = jnp.concatenate([jnp.where(left, g, zero), jnp.where(left, zero, g)], axis=0)
            first = l_ref[2 * p : 2 * p + 1, :]
            second = l_ref[2 * p + 1 : 2 * p + 2, :]
            if a == 0:
                logs = jnp.where(low, first, pltpu.roll(second, CL, 1))
            else:
                logs = jnp.where(low, pltpu.roll(first, CL, 1), second)
            scores = _dot(ks, qd, NT) * inv_root
            prob = jnp.exp(scores - logs)
            prob_grad = _dot(vs, gd, NT)
            delta = jnp.sum(prob * prob_grad, axis=0, keepdims=True)
            score_bf = (prob * (prob_grad - delta)).astype(BF16)
            prob_bf = prob.astype(BF16)
            key_cols.append((_dot(score_bf, qd) * inv_root).astype(BF16))
            value_cols.append(_dot(prob_bf, gd).astype(BF16))
            dq = (_dot(score_bf, ks, TN) * inv_root).astype(BF16)
            dq_ref[CL * a : CL * (a + 1), 2 * HD * p : 2 * HD * p + HD] = dq[:CL, :HD]
            dq_ref[CL * a : CL * (a + 1), 2 * HD * p + HD : 2 * HD * (p + 1)] = dq[CL:, HD:]
        key_parts.append(jnp.concatenate(key_cols, axis=1))
        value_parts.append(jnp.concatenate(value_cols, axis=1))
    key_grad = jnp.concatenate(key_parts, axis=0)
    value_grad = jnp.concatenate(value_parts, axis=0)
    half = (_dot(wk_ref[...], key_grad, NT) + _dot(wv_ref[...], value_grad, NT)).astype(BF16)
    for a in range(STEP):
        mine_ref[:, R * a : R * (a + 1)] = half[:, 2 * R * a : 2 * R * a + R]
        send_ref[:, R * a : R * (a + 1)] = half[:, 2 * R * a + R : 2 * R * (a + 1)]


def _span_call(first, steps, section, queries, grad_out, log_sums, neighbours, kw, vw, held):
    tokens, columns = queries.shape
    heads = log_sums.shape[0]
    whole = lambda i, s: (0, 0)
    rows = lambda i, s: (first + i, 0)
    in_specs = [
        pl.BlockSpec((STEP * CL, columns), rows),
        pl.BlockSpec((STEP * CL, columns), rows),
        pl.BlockSpec((heads, STEP * CL), lambda i, s: (0, first + i)),
        pl.BlockSpec((STEP, 2 * R, DE), lambda i, s: (first + i, 0, 0)),
        pl.BlockSpec((DE, columns), whole),
        pl.BlockSpec((DE, columns), whole),
    ]
    args = [queries, grad_out, log_sums, neighbours, kw, vw]
    aliases = {}
    if held is not None:
        in_specs.append(pl.BlockSpec(memory_space=pl.ANY))
        args.append(held)
        aliases = {len(args): 0}
    half_spec = pl.BlockSpec((DE, STEP * R), lambda i, s: (0, i))
    half_shape = jax.ShapeDtypeStruct((DE, steps * STEP * R), BF16)
    spans = steps * STEP
    return pl.pallas_call(
        _span_kernel,
        grid_spec=pltpu.PrefetchScalarGridSpec(
            num_scalar_prefetch=1,
            grid=(steps,),
            in_specs=in_specs,
            out_specs=[pl.BlockSpec((STEP * CL, columns), rows), half_spec, half_spec],
        ),
        out_shape=[jax.ShapeDtypeStruct((tokens, columns), BF16), half_shape, half_shape],
        input_output_aliases=aliases,
        compiler_params=pltpu.CompilerParams(vmem_limit_bytes=48 << 20),
        cost_estimate=pl.CostEstimate(
            flops=spans * 2 * R * columns * (8 * DE + 10 * CL),
            transcendentals=spans * 2 * R * CL * heads,
            bytes_accessed=4 * DE * columns + spans * 1000000,
        ),
    )(section, *args)


def _weight_kernel(order, spans, chunk_spans, ids_ref, *refs):
    got_refs = refs[: len(chunk_spans)]
    x_ref, out_ref, acc_ref, enc_ref = refs[len(chunk_spans) :]
    peers = got_refs[0].shape[0]
    blocks = acc_ref.shape[0]
    cols = acc_ref.shape[1]
    owned = blocks // peers
    low = lax.broadcasted_iota(jnp.int32, (cols, R), 1) < HR
    acc_ref[...] = jnp.zeros_like(acc_ref)

    def add_peer(src, carry):
        at = 0
        for got_ref, count in zip(got_refs, chunk_spans):
            for c in range(count):
                tile = got_ref[src, :, R * c : R * (c + 1)].astype(F32)
                base = src * (2 * spans) + 2 * (at + c)
                first = ids_ref[base]
                second = ids_ref[base + 1]
                acc_ref[first] += jnp.where(low, tile, 0.0)
                acc_ref[second] += jnp.where(low, 0.0, tile)
            at += count
        return carry

    lax.fori_loop(0, peers, add_peer, 0)
    for b in range(0, blocks, 2):
        even = acc_ref[b]
        odd = acc_ref[b + 1]
        even = even + pltpu.roll(even, HR, 1)
        odd = odd + pltpu.roll(odd, HR, 1)
        enc_ref[:, HR * b : HR * (b + 2)] = jnp.where(low, even, odd).astype(BF16)
    total = None
    for pos, owner in enumerate(order):
        lo = owner * owned * HR
        part = _dot(enc_ref[:, lo : lo + owned * HR], x_ref[pos, : owned * HR, :])
        total = part if total is None else total + part
    scale = (blocks * R) ** (-0.5)
    out_ref[...] = (total * scale).T


def _weight_call(order, spans, chunk_spans, ids, gots, x_all, blocks):
    cols = gots[0].shape[1]
    vmem = pl.BlockSpec(memory_space=pltpu.VMEM)
    return pl.pallas_call(
        functools.partial(_weight_kernel, order, spans, chunk_spans),
        in_specs=[pl.BlockSpec(memory_space=pltpu.SMEM)] + [vmem] * (len(gots) + 1),
        out_specs=vmem,
        out_shape=jax.ShapeDtypeStruct((DE, cols), F32),
        scratch_shapes=[
            pltpu.VMEM((blocks, cols, R), F32),
            pltpu.VMEM((cols, blocks * HR), BF16),
        ],
        compiler_params=pltpu.CompilerParams(vmem_limit_bytes=56 << 20),
        cost_estimate=pl.CostEstimate(
            flops=2 * cols * blocks * HR * DE, transcendentals=0, bytes_accessed=6000000
        ),
    )(ids, *gots, x_all)


def per_device(
    queries,
    grad_out,
    log_sums,
    neighbours,
    key_weight,
    value_weight,
    neighbour_ids,
    block_slot,
    enc_input,
):
    spans = neighbour_ids.shape[0]
    blocks = block_slot.shape[0]
    owned = enc_input.shape[0] // R
    peers = lax.axis_size("dp")
    section = lax.axis_index("section").astype(jnp.int32)
    order = (0, 2, 4, 6, 7, 5, 3, 1) if peers == 8 else tuple(range(peers))

    flat_ids = neighbour_ids.reshape(2 * spans)
    hit = flat_ids[:, None] == jnp.arange(blocks, dtype=jnp.int32)[None, :]
    storage = jnp.sum(jnp.where(hit, block_slot[None, :], 0), axis=1)
    id_rows = jnp.pad(storage.astype(BF16)[None, :], ((0, 7), (0, DE - 2 * spans)))
    x_half = lax.dynamic_index_in_dim(
        enc_input.reshape(owned, 2, HR, DE), section, 1, keepdims=False
    ).reshape(owned * HR, DE)
    x_all = lax.all_gather(
        jnp.concatenate([x_half, id_rows], axis=0),
        "dp",
        axis=0,
        tiled=False,
        axis_index_groups=[list(order)],
    )

    held = None
    gots = []
    first = 0
    swap = [(0, 1), (1, 0)]
    for steps in CHUNKS:
        held, mine, send = _span_call(
            first,
            steps,
            section[None],
            queries,
            grad_out,
            log_sums,
            neighbours,
            key_weight,
            value_weight,
            held,
        )
        other = lax.ppermute(send, "section", swap)
        ref_grad = (mine.astype(F32) + other.astype(F32)).astype(BF16)
        ref_grad = ref_grad.reshape(peers, DE // peers, steps * STEP * R)
        gots.append(lax.all_to_all(ref_grad, "dp", 0, 0, tiled=True))
        first += steps

    id_table = x_all[:, owned * HR, : 2 * spans].astype(jnp.int32)
    inverse = [order.index(d) for d in range(peers)]
    ids = jnp.concatenate([id_table[i] for i in inverse], axis=0)
    chunk_spans = tuple(n * STEP for n in CHUNKS)
    weight = _weight_call(order, spans, chunk_spans, ids, gots, x_all, blocks)
    rows = DE // (2 * peers)
    tiles = lax.all_to_all(
        weight.reshape(2 * peers, rows, DE // peers), ("dp", "section"), 0, 0, tiled=True
    )
    tiles = tiles.reshape(peers, 2, rows, DE // peers)
    weight_grad = jnp.transpose(tiles[:, 0] + tiles[:, 1], (1, 0, 2)).reshape(rows, DE)
    return (held, weight_grad)


def solution(mesh):
    return jax.shard_map(
        per_device,
        mesh=mesh,
        in_specs=(
            P(("group", "dp"), "section"),
            P(("group", "dp"), "section"),
            P("section", ("group", "dp")),
            P(("group", "dp"), None, None),
            P(None, "section"),
            P(None, "section"),
            P(("group", "dp"), None),
            P("group"),
            P(("group", "dp"), None),
        ),
        out_specs=(P(("group", "dp"), "section"), P(("group", "dp", "section"), None)),
        check_vma=False,
    )
```

```python
import functools

import jax
import jax.numpy as jnp
from jax import lax
from jax.experimental import pallas as pl
from jax.experimental.pallas import tpu as pltpu
from jax.sharding import PartitionSpec as P

HD = 128
DE = 896
CL = 64
R = 128
HR = R // 2
F32 = jnp.float32
BF16 = jnp.bfloat16
NT = (((1,), (1,)), ((), ()))
TN = (((0,), (0,)), ((), ()))


def _dot(a, b, dims=(((1,), (0,)), ((), ()))):
    return lax.dot_general(a, b, dims, preferred_element_type=F32)


def _span_kernel(first, spans, sec_ref, q_ref, g_ref, l_ref, n_ref, wk_ref, wv_ref, *rest):
    dq_ref, mine_ref, send_ref = rest[-3:]
    sec = sec_ref[0]
    inv_root = HD ** (-0.5)
    pairs = q_ref.shape[1] // (2 * HD)
    rows = []
    for a in range(spans):
        for half in range(2):
            for k in range(2):
                lo = k * R + half * HR
                rows.append(n_ref[a, lo : lo + HR, :])
    rows = jnp.concatenate(rows, axis=0)
    left = lax.broadcasted_iota(jnp.int32, (CL, 2 * HD), 1) < HD
    key_cols = [[] for _ in range(spans)]
    value_cols = [[] for _ in range(spans)]
    for p in range(pairs):
        cols = slice(2 * HD * p, 2 * HD * (p + 1))
        keys = _dot(rows, wk_ref[:, cols]).astype(BF16)
        values = _dot(rows, wv_ref[:, cols]).astype(BF16)
        for a in range(spans):
            ks = keys[2 * R * a : 2 * R * (a + 1)]
            vs = values[2 * R * a : 2 * R * (a + 1)]
            q = q_ref[CL * a : CL * (a + 1), cols]
            g = g_ref[CL * a : CL * (a + 1), cols]
            zero = jnp.zeros_like(q)
            qd = jnp.concatenate([jnp.where(left, q, zero), jnp.where(left, zero, q)], axis=0)
            gd = jnp.concatenate([jnp.where(left, g, zero), jnp.where(left, zero, g)], axis=0)
            at = slice(CL * (first + a), CL * (first + a + 1))
            logs = jnp.concatenate(
                [l_ref[2 * p : 2 * p + 1, at], l_ref[2 * p + 1 : 2 * p + 2, at]], axis=1
            )
            prob = jnp.exp(_dot(ks, qd, NT) * inv_root - logs)
            prob_grad = _dot(vs, gd, NT)
            delta = jnp.sum(prob * prob_grad, axis=0, keepdims=True)
            score_bf = (prob * (prob_grad - delta)).astype(BF16)
            prob_bf = prob.astype(BF16)
            key_cols[a].append((_dot(score_bf, qd) * inv_root).astype(BF16))
            value_cols[a].append(_dot(prob_bf, gd).astype(BF16))
            dq = (_dot(score_bf, ks, TN) * inv_root).astype(BF16)
            dq_ref[CL * a : CL * (a + 1), 2 * HD * p : 2 * HD * p + HD] = dq[:CL, :HD]
            dq_ref[CL * a : CL * (a + 1), 2 * HD * p + HD : 2 * HD * (p + 1)] = dq[CL:, HD:]
    width = DE // 2
    for a in range(spans):
        key_grad = jnp.concatenate(key_cols[a], axis=1)
        value_grad = jnp.concatenate(value_cols[a], axis=1)
        for lane, out_ref in ((sec, mine_ref), (1 - sec, send_ref)):
            at = pl.ds(pl.multiple_of(lane * width, width), width)
            part = _dot(wk_ref[at, :], key_grad, NT) + _dot(wv_ref[at, :], value_grad, NT)
            part = part.astype(BF16)
            for half in range(2):
                out_ref[half, :, R * a : R * (a + 1)] = part[:, half * R : (half + 1) * R]


def _span_call(first, spans, section, queries, grad_out, log_sums, neighbours, kw, vw, held):
    tokens, columns = queries.shape
    heads = log_sums.shape[0]
    whole = lambda i, s: (0, 0)
    block = first // spans
    in_specs = [
        pl.BlockSpec((spans * CL, columns), lambda i, s: (block, 0)),
        pl.BlockSpec((spans * CL, columns), lambda i, s: (block, 0)),
        pl.BlockSpec((heads, tokens), whole),
        pl.BlockSpec((spans, 2 * R, DE), lambda i, s: (block, 0, 0)),
        pl.BlockSpec((DE, columns), whole),
        pl.BlockSpec((DE, columns), whole),
    ]
    args = [queries, grad_out, log_sums, neighbours, kw, vw]
    args = [pltpu.with_memory_space_constraint(x, pltpu.HBM) for x in args]
    aliases = {}
    if held is not None:
        in_specs.append(pl.BlockSpec(memory_space=pl.ANY))
        args.append(held)
        aliases = {len(args): 0}
    half_spec = pl.BlockSpec((2, DE // 2, spans * R), lambda i, s: (0, 0, 0))
    half_shape = jax.ShapeDtypeStruct((2, DE // 2, spans * R), BF16)
    return pl.pallas_call(
        functools.partial(_span_kernel, first, spans),
        grid_spec=pltpu.PrefetchScalarGridSpec(
            num_scalar_prefetch=1,
            grid=(1,),
            in_specs=in_specs,
            out_specs=[
                pl.BlockSpec((spans * CL, columns), lambda i, s: (block, 0)),
                half_spec,
                half_spec,
            ],
        ),
        out_shape=[jax.ShapeDtypeStruct((tokens, columns), BF16), half_shape, half_shape],
        input_output_aliases=aliases,
        compiler_params=pltpu.CompilerParams(vmem_limit_bytes=48 << 20),
        cost_estimate=pl.CostEstimate(
            flops=spans * 2 * R * columns * (8 * DE + 10 * CL),
            transcendentals=spans * 2 * R * CL * heads,
            bytes_accessed=4 * DE * columns + spans * 1000000,
        ),
    )(section, *args)


def _scatter(got, src, count, peers, spans, first, place_ref, ids_ref, slot_ref, acc_ref):
    inner = peers // 2
    low = lax.broadcasted_iota(jnp.int32, acc_ref.shape[1:], 1) < HR
    turn = jnp.bitwise_xor(src % inner, place_ref[1])
    side = jnp.bitwise_xor(src // inner, place_ref[0])
    at = ((2 * turn + side) * spans + first) * 2
    for c in range(count):
        tile = got[src, :, R * c : R * (c + 1)].astype(F32)
        left = slot_ref[ids_ref[at + 2 * c]]
        right = slot_ref[ids_ref[at + 2 * c + 1]]
        acc_ref[left] += jnp.where(low, tile, 0.0)
        acc_ref[right] += jnp.where(low, 0.0, tile)


def _weight_kernel(spans, chunks, place_ref, ids_ref, slot_ref, *refs):
    n_gots = len(chunks)
    n_xs = len(refs) - 5 - 2 * n_gots
    got_hbm, x_hbm = refs[:n_gots], refs[n_gots : n_gots + n_xs]
    out_ref, acc_ref, enc_ref = refs[n_gots + n_xs : n_gots + n_xs + 3]
    gots = refs[n_gots + n_xs + 3 : 2 * n_gots + n_xs + 3]
    x_refs, sems = refs[-2], refs[-1]
    peers = gots[0].shape[0]
    blocks, cols = acc_ref.shape[:2]
    owned = blocks // peers
    inner = peers // 2
    upper, lower, sec = place_ref[0], place_ref[1], place_ref[2]
    share = owned // 2
    rows = share * HR

    got_copies = [pltpu.make_async_copy(got_hbm[n], gots[n], sems.at[n]) for n in range(n_gots)]
    x_copies = []
    for n in range(n_xs):
        to = x_refs.at[n // 2, (n % 2) * rows : (n % 2 + 1) * rows, :]
        x_copies.append(pltpu.make_async_copy(x_hbm[n].at[:rows, :], to, sems.at[n_gots + n]))
    for copy in got_copies + x_copies:
        copy.start()
    acc_ref[...] = jnp.zeros_like(acc_ref)
    first = 0
    for n, count in enumerate(chunks):
        got_copies[n].wait()

        def add_peer(src, carry, n=n, count=count, first=first):
            _scatter(
                gots[n], src, count, peers, spans, first, place_ref, ids_ref, slot_ref, acc_ref
            )
            return carry

        lax.fori_loop(0, peers, add_peer, 0)
        first += count
    low = lax.broadcasted_iota(jnp.int32, (cols, R), 1) < HR
    total = None
    for turn in range(inner):
        for far in range(2):
            n = 2 * turn + far
            near_sec = 1 - sec if far else sec
            for side in range(2):
                owner = jnp.bitwise_xor(lower, turn) + inner * (1 - upper if side else upper)
                base = owner * owned + near_sec * share
                for b in range(0, share, 2):
                    even = acc_ref[base + b]
                    odd = acc_ref[base + b + 1]
                    even = even + pltpu.roll(even, HR, 1)
                    odd = odd + pltpu.roll(odd, HR, 1)
                    lo = side * rows + b * HR
                    enc_ref[n, :, lo : lo + 2 * HR] = jnp.where(low, even, odd).astype(BF16)
            x_copies[2 * n].wait()
            x_copies[2 * n + 1].wait()
            part = _dot(enc_ref[n], x_refs[n])
            total = part if total is None else total + part
    scale = (blocks * R) ** (-0.5)
    out_ref[...] = (total * scale).T


def _weight_call(spans, chunks, place, ids, slots, gots, xs):
    cols = gots[0].shape[1]
    blocks = slots.shape[0]
    owned = blocks // gots[0].shape[0]
    smem = pl.BlockSpec(memory_space=pltpu.SMEM)
    anywhere = pl.BlockSpec(memory_space=pl.ANY)
    large = [pltpu.with_memory_space_constraint(x, pltpu.HBM) for x in [*gots, *xs]]
    pairs = len(xs) // 2
    return pl.pallas_call(
        functools.partial(_weight_kernel, spans, chunks),
        in_specs=[smem] * 3 + [anywhere] * len(large),
        out_specs=pl.BlockSpec(memory_space=pltpu.VMEM),
        out_shape=jax.ShapeDtypeStruct((DE, cols), F32),
        scratch_shapes=[
            pltpu.VMEM((blocks, cols, R), F32),
            pltpu.VMEM((pairs, cols, owned * HR), BF16),
        ]
        + [pltpu.VMEM(x.shape, BF16) for x in gots]
        + [
            pltpu.VMEM((pairs, owned * HR, DE), BF16),
            pltpu.SemaphoreType.DMA((len(large),)),
        ],
        compiler_params=pltpu.CompilerParams(vmem_limit_bytes=40 << 20),
        cost_estimate=pl.CostEstimate(
            flops=2 * cols * blocks * HR * DE, transcendentals=0, bytes_accessed=6000000
        ),
    )(place, ids, slots, *large)


def per_device(
    queries,
    grad_out,
    log_sums,
    neighbours,
    key_weight,
    value_weight,
    neighbour_ids,
    block_slot,
    enc_input,
):
    spans = neighbour_ids.shape[0]
    owned = enc_input.shape[0] // R
    peers = lax.axis_size("dp")
    inner = peers // 2
    section = lax.axis_index("section").astype(jnp.int32)
    index = lax.axis_index("dp").astype(jnp.int32)
    upper, lower = index // inner, index % inner
    swap = [(0, 1), (1, 0)]

    id_rows = jnp.pad(neighbour_ids.astype(BF16), ((0, -spans % 8), (0, DE - 2)))
    split = enc_input.reshape(2, owned // 2, 2, HR, DE)
    split = lax.dynamic_index_in_dim(split, section, 0, keepdims=False)
    own = lax.dynamic_index_in_dim(split, upper, 1, keepdims=False)
    own = jnp.concatenate([own.reshape(owned // 2 * HR, DE), id_rows], axis=0)
    away = lax.dynamic_index_in_dim(split, 1 - upper, 1, keepdims=False)
    away = jnp.concatenate([away.reshape(owned // 2 * HR, DE), id_rows], axis=0)
    mirror = lax.ppermute(away, "dp", [(i, i ^ inner) for i in range(peers)])

    def spread(pack):
        return [pack] + [
            lax.ppermute(pack, "dp", [(i, i ^ m) for i in range(peers)]) for m in range(1, inner)
        ]

    own = spread(own)
    held = None
    gots = []
    first = 0
    chunks = (spans // 2, spans - spans // 2)
    for count in chunks:
        held, mine, send = _span_call(
            first,
            count,
            section[None],
            queries,
            grad_out,
            log_sums,
            neighbours,
            key_weight,
            value_weight,
            held,
        )
        if not gots:
            mirror, own, send = lax.optimization_barrier((mirror, own, send))
        other = lax.ppermute(send, "section", swap)
        if gots:
            gots[-1], other = lax.optimization_barrier((gots[-1], other))
        ref_grad = (mine.astype(F32) + other.astype(F32)).astype(BF16)
        ref_grad = ref_grad.reshape(peers, DE // peers, count * R)
        held, mirror, ref_grad = lax.optimization_barrier((held, mirror, ref_grad))
        gots.append(lax.all_to_all(ref_grad, "dp", 0, 0, tiled=True))
        first += count

    packs = spread(mirror)
    xs = []
    for pair in zip(own, packs):
        xs += list(pair) + [lax.ppermute(x, "section", swap) for x in pair]
    cut = owned // 2 * HR
    ids = [x[cut : cut + spans, :2] for pair in zip(own, packs) for x in pair]
    ids = jnp.concatenate(ids, axis=0).astype(jnp.int32)
    place = jnp.stack([upper, lower, section])
    weight = _weight_call(
        spans, chunks, place, ids.reshape(-1), block_slot, gots, xs
    )
    rows = DE // (2 * peers)
    cols = DE // peers
    tiles = lax.all_to_all(weight.reshape(2 * peers, rows, cols), ("dp", "section"), 0, 0, tiled=True)
    tiles = tiles.reshape(2, inner, 2, rows, cols)
    weight_grad = jnp.transpose(tiles[0] + tiles[1], (2, 1, 0, 3)).reshape(rows, DE)
    return (held, weight_grad)


def solution(mesh):
    return jax.shard_map(
        per_device,
        mesh=mesh,
        in_specs=(
            P(("group", "dp"), "section"),
            P(("group", "dp"), "section"),
            P("section", ("group", "dp")),
            P(("group", "dp"), None, None),
            P(None, "section"),
            P(None, "section"),
            P(("group", "dp"), None),
            P("group"),
            P(("group", "dp"), None),
        ),
        out_specs=(P(("group", "dp"), "section"), P(("group", "dp", "section"), None)),
        check_vma=False,
    )
```

```python
import functools

import jax
import jax.numpy as jnp
from jax import lax
from jax.experimental import pallas as pl
from jax.experimental.pallas import tpu as pltpu
from jax.sharding import PartitionSpec as P

HD = 128
DE = 896
CL = 64
R = 128
HR = R // 2
COST = 1 << 36
F32 = jnp.float32
BF16 = jnp.bfloat16
NT = (((1,), (1,)), ((), ()))
TN = (((0,), (0,)), ((), ()))


def _dot(a, b, dims=(((1,), (0,)), ((), ()))):
    return lax.dot_general(a, b, dims, preferred_element_type=F32)


def _span_kernel(first, spans, sec_ref, q_ref, g_ref, l_ref, n_ref, wk_ref, wv_ref, *rest):
    dq_ref, mine_ref, send_ref = rest[-3:]
    sec = sec_ref[0]
    inv_root = HD ** (-0.5)
    pairs = q_ref.shape[1] // (2 * HD)
    rows = []
    for a in range(spans):
        for half in range(2):
            for k in range(2):
                lo = k * R + half * HR
                rows.append(n_ref[a, lo : lo + HR, :])
    rows = jnp.concatenate(rows, axis=0)
    left = lax.broadcasted_iota(jnp.int32, (CL, 2 * HD), 1) < HD
    key_cols = [[] for _ in range(spans)]
    value_cols = [[] for _ in range(spans)]
    for p in range(pairs):
        cols = slice(2 * HD * p, 2 * HD * (p + 1))
        keys = _dot(rows, wk_ref[:, cols]).astype(BF16)
        values = _dot(rows, wv_ref[:, cols]).astype(BF16)
        for a in range(spans):
            ks = keys[2 * R * a : 2 * R * (a + 1)]
            vs = values[2 * R * a : 2 * R * (a + 1)]
            q = q_ref[CL * a : CL * (a + 1), cols]
            g = g_ref[CL * a : CL * (a + 1), cols]
            zero = jnp.zeros_like(q)
            qd = jnp.concatenate([jnp.where(left, q, zero), jnp.where(left, zero, q)], axis=0)
            gd = jnp.concatenate([jnp.where(left, g, zero), jnp.where(left, zero, g)], axis=0)
            at = slice(CL * (first + a), CL * (first + a + 1))
            logs = jnp.concatenate(
                [l_ref[2 * p : 2 * p + 1, at], l_ref[2 * p + 1 : 2 * p + 2, at]], axis=1
            )
            prob = jnp.exp(_dot(ks, qd, NT) * inv_root - logs)
            prob_grad = _dot(vs, gd, NT)
            delta = jnp.sum(prob * prob_grad, axis=0, keepdims=True)
            score_bf = (prob * (prob_grad - delta)).astype(BF16)
            prob_bf = prob.astype(BF16)
            key_cols[a].append((_dot(score_bf, qd) * inv_root).astype(BF16))
            value_cols[a].append(_dot(prob_bf, gd).astype(BF16))
            dq = (_dot(score_bf, ks, TN) * inv_root).astype(BF16)
            dq_ref[CL * a : CL * (a + 1), 2 * HD * p : 2 * HD * p + HD] = dq[:CL, :HD]
            dq_ref[CL * a : CL * (a + 1), 2 * HD * p + HD : 2 * HD * (p + 1)] = dq[CL:, HD:]
    width = DE // 2
    for a in range(spans):
        key_grad = jnp.concatenate(key_cols[a], axis=1)
        value_grad = jnp.concatenate(value_cols[a], axis=1)
        for lane, out_ref in ((sec, mine_ref), (1 - sec, send_ref)):
            at = pl.ds(pl.multiple_of(lane * width, width), width)
            part = _dot(wk_ref[at, :], key_grad, NT) + _dot(wv_ref[at, :], value_grad, NT)
            part = part.astype(BF16)
            for half in range(2):
                out_ref[half, :, R * a : R * (a + 1)] = part[:, half * R : (half + 1) * R]


def _span_call(first, spans, section, queries, grad_out, log_sums, neighbours, kw, vw, held):
    tokens, columns = queries.shape
    heads = log_sums.shape[0]
    whole = lambda i, s: (0, 0)
    block = first // spans
    in_specs = [
        pl.BlockSpec((spans * CL, columns), lambda i, s: (block, 0)),
        pl.BlockSpec((spans * CL, columns), lambda i, s: (block, 0)),
        pl.BlockSpec((heads, tokens), whole),
        pl.BlockSpec((spans, 2 * R, DE), lambda i, s: (block, 0, 0)),
        pl.BlockSpec((DE, columns), whole),
        pl.BlockSpec((DE, columns), whole),
    ]
    args = [queries, grad_out, log_sums, neighbours, kw, vw]
    args = [pltpu.with_memory_space_constraint(x, pltpu.HBM) for x in args]
    aliases = {}
    if held is not None:
        in_specs.append(pl.BlockSpec(memory_space=pl.ANY))
        args.append(held)
        aliases = {len(args): 0}
    half_spec = pl.BlockSpec((2, DE // 2, spans * R), lambda i, s: (0, 0, 0))
    half_shape = jax.ShapeDtypeStruct((2, DE // 2, spans * R), BF16)
    return pl.pallas_call(
        functools.partial(_span_kernel, first, spans),
        grid_spec=pltpu.PrefetchScalarGridSpec(
            num_scalar_prefetch=1,
            grid=(1,),
            in_specs=in_specs,
            out_specs=[
                pl.BlockSpec((spans * CL, columns), lambda i, s: (block, 0)),
                half_spec,
                half_spec,
            ],
        ),
        out_shape=[jax.ShapeDtypeStruct((tokens, columns), BF16), half_shape, half_shape],
        input_output_aliases=aliases,
        compiler_params=pltpu.CompilerParams(vmem_limit_bytes=48 << 20),
        cost_estimate=pl.CostEstimate(
            flops=spans * 2 * R * columns * (8 * DE + 10 * CL),
            transcendentals=spans * 2 * R * CL * heads,
            bytes_accessed=4 * DE * columns + spans * 1000000,
        ),
    )(section, *args)


def _ids_kernel(*refs):
    out_ref = refs[-1]
    for n, x_ref in enumerate(refs[:-1]):
        table = x_ref[...].astype(F32).astype(jnp.int32)
        out_ref[2 * n : 2 * n + 2, :] = table[:2, :]


def _ids_call(packs, start, rows):
    spec = pl.BlockSpec((rows, R), lambda i: (start // rows, 0))
    return pl.pallas_call(
        _ids_kernel,
        grid=(1,),
        in_specs=[spec] * len(packs),
        out_specs=pl.BlockSpec((2 * len(packs), R), lambda i: (0, 0)),
        out_shape=jax.ShapeDtypeStruct((2 * len(packs), R), jnp.int32),
        cost_estimate=pl.CostEstimate(flops=COST, transcendentals=0, bytes_accessed=1000),
    )(*packs)


def _scatter(got, src, count, peers, spans, first, place_ref, ids_ref, slot_ref, acc_ref):
    inner = peers // 2
    low = lax.broadcasted_iota(jnp.int32, acc_ref.shape[1:], 1) < HR
    turn = jnp.bitwise_xor(src % inner, place_ref[1])
    side = jnp.bitwise_xor(src // inner, place_ref[0])
    at = (2 * turn + side) * 2
    for c in range(count):
        tile = got[src, :, R * c : R * (c + 1)].astype(F32)
        left = slot_ref[ids_ref[at, first + c]]
        right = slot_ref[ids_ref[at + 1, first + c]]
        acc_ref[left] += jnp.where(low, tile, 0.0)
        acc_ref[right] += jnp.where(low, 0.0, tile)


def _add_kernel(count, spans, first, place_ref, ids_ref, slot_ref, got_ref, acc_ref):
    peers = got_ref.shape[0]
    acc_ref[...] = jnp.zeros_like(acc_ref)

    def add_peer(src, carry):
        _scatter(
            got_ref, src, count, peers, spans, first, place_ref, ids_ref, slot_ref, acc_ref
        )
        return carry

    lax.fori_loop(0, peers, add_peer, 0)


def _add_call(count, spans, first, place, ids, slots, got):
    smem = pl.BlockSpec(memory_space=pltpu.SMEM)
    vmem = pl.BlockSpec(memory_space=pltpu.VMEM)
    return pl.pallas_call(
        functools.partial(_add_kernel, count, spans, first),
        in_specs=[smem] * 3 + [vmem],
        out_specs=vmem,
        out_shape=jax.ShapeDtypeStruct((slots.shape[0], got.shape[1], R), F32),
        compiler_params=pltpu.CompilerParams(vmem_limit_bytes=16 << 20),
        cost_estimate=pl.CostEstimate(flops=1000, transcendentals=0, bytes_accessed=1000),
    )(place, ids, slots, got)


def _weight_kernel(count, spans, first, place_ref, ids_ref, slot_ref, got_ref, sum_ref, *refs):
    x_hbm = refs[:-5]
    out_ref, acc_ref, enc_ref, x_refs, sems = refs[-5:]
    peers = got_ref.shape[0]
    blocks, cols = acc_ref.shape[:2]
    owned = blocks // peers
    inner = peers // 2
    upper, lower, sec = place_ref[0], place_ref[1], place_ref[2]
    share = owned // 2
    rows = share * HR

    x_copies = []
    for n in range(len(x_hbm)):
        to = x_refs.at[n // 2, (n % 2) * rows : (n % 2 + 1) * rows, :]
        x_copies.append(pltpu.make_async_copy(x_hbm[n].at[:rows, :], to, sems.at[n]))
    for copy in x_copies:
        copy.start()
    acc_ref[...] = sum_ref[...]

    def add_peer(src, carry):
        _scatter(
            got_ref, src, count, peers, spans, first, place_ref, ids_ref, slot_ref, acc_ref
        )
        return carry

    lax.fori_loop(0, peers, add_peer, 0)
    low = lax.broadcasted_iota(jnp.int32, (cols, R), 1) < HR
    total = None
    for turn in range(inner):
        for far in range(2):
            n = 2 * turn + far
            near_sec = 1 - sec if far else sec
            for side in range(2):
                owner = jnp.bitwise_xor(lower, turn) + inner * (1 - upper if side else upper)
                base = owner * owned + near_sec * share
                for b in range(0, share, 2):
                    even = acc_ref[base + b]
                    odd = acc_ref[base + b + 1]
                    even = even + pltpu.roll(even, HR, 1)
                    odd = odd + pltpu.roll(odd, HR, 1)
                    lo = side * rows + b * HR
                    enc_ref[n, :, lo : lo + 2 * HR] = jnp.where(low, even, odd).astype(BF16)
            x_copies[2 * n].wait()
            x_copies[2 * n + 1].wait()
            part = _dot(enc_ref[n], x_refs[n])
            total = part if total is None else total + part
    scale = (blocks * R) ** (-0.5)
    out_ref[...] = (total * scale).T


def _weight_call(count, spans, first, place, ids, slots, got, partial_sum, xs):
    cols = got.shape[1]
    blocks = slots.shape[0]
    owned = blocks // got.shape[0]
    smem = pl.BlockSpec(memory_space=pltpu.SMEM)
    vmem = pl.BlockSpec(memory_space=pltpu.VMEM)
    xs = [pltpu.with_memory_space_constraint(x, pltpu.HBM) for x in xs]
    pairs = len(xs) // 2
    return pl.pallas_call(
        functools.partial(_weight_kernel, count, spans, first),
        in_specs=[smem] * 3 + [vmem] * 2 + [pl.BlockSpec(memory_space=pl.ANY)] * len(xs),
        out_specs=vmem,
        out_shape=jax.ShapeDtypeStruct((DE, cols), F32),
        scratch_shapes=[
            pltpu.VMEM((blocks, cols, R), F32),
            pltpu.VMEM((pairs, cols, owned * HR), BF16),
            pltpu.VMEM((pairs, owned * HR, DE), BF16),
            pltpu.SemaphoreType.DMA((len(xs),)),
        ],
        compiler_params=pltpu.CompilerParams(vmem_limit_bytes=32 << 20),
        cost_estimate=pl.CostEstimate(
            flops=2 * cols * blocks * HR * DE, transcendentals=0, bytes_accessed=6000000
        ),
    )(place, ids, slots, got, partial_sum, *xs)


def per_device(
    queries,
    grad_out,
    log_sums,
    neighbours,
    key_weight,
    value_weight,
    neighbour_ids,
    block_slot,
    enc_input,
):
    spans = neighbour_ids.shape[0]
    owned = enc_input.shape[0] // R
    peers = lax.axis_size("dp")
    inner = peers // 2
    section = lax.axis_index("section").astype(jnp.int32)
    index = lax.axis_index("dp").astype(jnp.int32)
    upper, lower = index // inner, index % inner
    swap = [(0, 1), (1, 0)]

    id_rows = jnp.pad(neighbour_ids.T.astype(BF16), ((0, 6), (0, DE - spans)))
    split = enc_input.reshape(2, owned // 2, 2, HR, DE)
    split = lax.dynamic_index_in_dim(split, section, 0, keepdims=False)
    own = lax.dynamic_index_in_dim(split, upper, 1, keepdims=False)
    own = jnp.concatenate([own.reshape(owned // 2 * HR, DE), id_rows], axis=0)
    away = lax.dynamic_index_in_dim(split, 1 - upper, 1, keepdims=False)
    away = jnp.concatenate([away.reshape(owned // 2 * HR, DE), id_rows], axis=0)
    mirror = lax.ppermute(away, "dp", [(i, i ^ inner) for i in range(peers)])

    def spread(pack):
        return [pack] + [
            lax.ppermute(pack, "dp", [(i, i ^ m) for i in range(peers)]) for m in range(1, inner)
        ]

    own = spread(own)
    held = None
    gots = []
    first = 0
    chunks = (spans // 2, spans - spans // 2)
    for count in chunks:
        held, mine, send = _span_call(
            first,
            count,
            section[None],
            queries,
            grad_out,
            log_sums,
            neighbours,
            key_weight,
            value_weight,
            held,
        )
        if not gots:
            mirror, own, send = lax.optimization_barrier((mirror, own, send))
        else:
            mirror, send = lax.optimization_barrier((mirror, send))
        other = lax.ppermute(send, "section", swap)
        if gots:
            gots[-1], other = lax.optimization_barrier((gots[-1], other))
        ref_grad = (mine.astype(F32) + other.astype(F32)).astype(BF16)
        ref_grad = ref_grad.reshape(peers, DE // peers, count * R)
        if not gots:
            held, ref_grad = lax.optimization_barrier((held, ref_grad))
        gots.append(lax.all_to_all(ref_grad, "dp", 0, 0, tiled=True))
        first += count

    packs = spread(mirror)
    xs = []
    for pair in zip(own, packs):
        xs += list(pair) + [lax.ppermute(x, "section", swap) for x in pair]
    pairs = [x for pair in zip(own, packs) for x in pair]
    ids = _ids_call(pairs, owned // 2 * HR, id_rows.shape[0])
    place = jnp.stack([upper, lower, section])
    ids = pltpu.with_memory_space_constraint(ids, pltpu.HBM)
    partial_sum = _add_call(chunks[0], spans, 0, place, ids, block_slot, gots[0])
    weight = _weight_call(
        chunks[1], spans, chunks[0], place, ids, block_slot, gots[1], partial_sum, xs
    )
    rows = DE // (2 * peers)
    cols = DE // peers
    tiles = lax.all_to_all(weight.reshape(2 * peers, rows, cols), ("dp", "section"), 0, 0, tiled=True)
    tiles = tiles.reshape(2, inner, 2, rows, cols)
    weight_grad = jnp.transpose(tiles[0] + tiles[1], (2, 1, 0, 3)).reshape(rows, DE)
    return (held, weight_grad)


def solution(mesh):
    return jax.shard_map(
        per_device,
        mesh=mesh,
        in_specs=(
            P(("group", "dp"), "section"),
            P(("group", "dp"), "section"),
            P("section", ("group", "dp")),
            P(("group", "dp"), None, None),
            P(None, "section"),
            P(None, "section"),
            P(("group", "dp"), None),
            P("group"),
            P(("group", "dp"), None),
        ),
        out_specs=(P(("group", "dp"), "section"), P(("group", "dp", "section"), None)),
        check_vma=False,
    )
```

```python
import functools

import jax
import jax.numpy as jnp
from jax import lax
from jax.experimental import pallas as pl
from jax.experimental.pallas import tpu as pltpu
from jax.sharding import PartitionSpec as P

HD = 128
DE = 896
CL = 64
R = 128
HR = R // 2
COST = 1 << 36
F32 = jnp.float32
BF16 = jnp.bfloat16
NT = (((1,), (1,)), ((), ()))
TN = (((0,), (0,)), ((), ()))


def _dot(a, b, dims=(((1,), (0,)), ((), ()))):
    return lax.dot_general(a, b, dims, preferred_element_type=F32)


def _span_kernel(first, spans, sec_ref, q_ref, g_ref, l_ref, n_ref, wk_ref, wv_ref, *rest):
    dq_ref, mine_ref, send_ref = rest[-3:]
    sec = sec_ref[0]
    inv_root = HD ** (-0.5)
    pairs = q_ref.shape[1] // (2 * HD)
    rows = []
    for a in range(spans):
        for half in range(2):
            for k in range(2):
                lo = k * R + half * HR
                rows.append(n_ref[a, lo : lo + HR, :])
    rows = jnp.concatenate(rows, axis=0)
    left = lax.broadcasted_iota(jnp.int32, (CL, 2 * HD), 1) < HD
    key_cols = [[] for _ in range(spans)]
    value_cols = [[] for _ in range(spans)]
    for p in range(pairs):
        cols = slice(2 * HD * p, 2 * HD * (p + 1))
        keys = _dot(rows, wk_ref[:, cols]).astype(BF16)
        values = _dot(rows, wv_ref[:, cols]).astype(BF16)
        for a in range(spans):
            ks = keys[2 * R * a : 2 * R * (a + 1)]
            vs = values[2 * R * a : 2 * R * (a + 1)]
            q = q_ref[CL * a : CL * (a + 1), cols]
            g = g_ref[CL * a : CL * (a + 1), cols]
            zero = jnp.zeros_like(q)
            qd = jnp.concatenate([jnp.where(left, q, zero), jnp.where(left, zero, q)], axis=0)
            gd = jnp.concatenate([jnp.where(left, g, zero), jnp.where(left, zero, g)], axis=0)
            at = slice(CL * (first + a), CL * (first + a + 1))
            logs = jnp.concatenate(
                [l_ref[2 * p : 2 * p + 1, at], l_ref[2 * p + 1 : 2 * p + 2, at]], axis=1
            )
            prob = jnp.exp(_dot(ks, qd, NT) * inv_root - logs)
            prob_grad = _dot(vs, gd, NT)
            delta = jnp.sum(prob * prob_grad, axis=0, keepdims=True)
            score_bf = (prob * (prob_grad - delta)).astype(BF16)
            prob_bf = prob.astype(BF16)
            key_cols[a].append((_dot(score_bf, qd) * inv_root).astype(BF16))
            value_cols[a].append(_dot(prob_bf, gd).astype(BF16))
            dq = (_dot(score_bf, ks, TN) * inv_root).astype(BF16)
            dq_ref[CL * a : CL * (a + 1), 2 * HD * p : 2 * HD * p + HD] = dq[:CL, :HD]
            dq_ref[CL * a : CL * (a + 1), 2 * HD * p + HD : 2 * HD * (p + 1)] = dq[CL:, HD:]
    width = DE // 2
    for a in range(spans):
        key_grad = jnp.concatenate(key_cols[a], axis=1)
        value_grad = jnp.concatenate(value_cols[a], axis=1)
        for lane, out_ref in ((sec, mine_ref), (1 - sec, send_ref)):
            at = pl.ds(pl.multiple_of(lane * width, width), width)
            part = _dot(wk_ref[at, :], key_grad, NT) + _dot(wv_ref[at, :], value_grad, NT)
            part = part.astype(BF16)
            for half in range(2):
                out_ref[half, :, R * a : R * (a + 1)] = part[:, half * R : (half + 1) * R]


def _span_call(first, spans, section, queries, grad_out, log_sums, neighbours, kw, vw, held):
    tokens, columns = queries.shape
    heads = log_sums.shape[0]
    whole = lambda i, s: (0, 0)
    block = first // spans
    in_specs = [
        pl.BlockSpec((spans * CL, columns), lambda i, s: (block, 0)),
        pl.BlockSpec((spans * CL, columns), lambda i, s: (block, 0)),
        pl.BlockSpec((heads, tokens), whole),
        pl.BlockSpec((spans, 2 * R, DE), lambda i, s: (block, 0, 0)),
        pl.BlockSpec((DE, columns), whole),
        pl.BlockSpec((DE, columns), whole),
    ]
    args = [queries, grad_out, log_sums, neighbours, kw, vw]
    args = [pltpu.with_memory_space_constraint(x, pltpu.HBM) for x in args]
    aliases = {}
    if held is not None:
        in_specs.append(pl.BlockSpec(memory_space=pl.ANY))
        args.append(held)
        aliases = {len(args): 0}
    half_spec = pl.BlockSpec((2, DE // 2, spans * R), lambda i, s: (0, 0, 0))
    half_shape = jax.ShapeDtypeStruct((2, DE // 2, spans * R), BF16)
    return pl.pallas_call(
        functools.partial(_span_kernel, first, spans),
        grid_spec=pltpu.PrefetchScalarGridSpec(
            num_scalar_prefetch=1,
            grid=(1,),
            in_specs=in_specs,
            out_specs=[
                pl.BlockSpec((spans * CL, columns), lambda i, s: (block, 0)),
                half_spec,
                half_spec,
            ],
        ),
        out_shape=[jax.ShapeDtypeStruct((tokens, columns), BF16), half_shape, half_shape],
        input_output_aliases=aliases,
        compiler_params=pltpu.CompilerParams(vmem_limit_bytes=48 << 20),
        cost_estimate=pl.CostEstimate(
            flops=spans * 2 * R * columns * (8 * DE + 10 * CL),
            transcendentals=spans * 2 * R * CL * heads,
            bytes_accessed=4 * DE * columns + spans * 1000000,
        ),
    )(section, *args)


def _ids_kernel(*refs):
    out_ref = refs[-1]
    for n, x_ref in enumerate(refs[:-1]):
        table = x_ref[...].astype(F32).astype(jnp.int32)
        out_ref[2 * n : 2 * n + 2, :] = table[:2, :]


def _ids_call(packs, start, rows):
    spec = pl.BlockSpec((rows, R), lambda i: (start // rows, 0))
    return pl.pallas_call(
        _ids_kernel,
        grid=(1,),
        in_specs=[spec] * len(packs),
        out_specs=pl.BlockSpec((2 * len(packs), R), lambda i: (0, 0)),
        out_shape=jax.ShapeDtypeStruct((2 * len(packs), R), jnp.int32),
        cost_estimate=pl.CostEstimate(flops=COST, transcendentals=0, bytes_accessed=1000),
    )(*packs)


def _scatter(got, src, count, peers, spans, first, place_ref, ids_ref, slot_ref, acc_ref):
    inner = peers // 2
    low = lax.broadcasted_iota(jnp.int32, acc_ref.shape[1:], 1) < HR
    turn = jnp.bitwise_xor(src % inner, place_ref[1])
    side = jnp.bitwise_xor(src // inner, place_ref[0])
    at = (2 * turn + side) * 2
    for c in range(count):
        tile = got[src, :, R * c : R * (c + 1)].astype(F32)
        left = slot_ref[ids_ref[at, first + c]]
        right = slot_ref[ids_ref[at + 1, first + c]]
        acc_ref[left] += jnp.where(low, tile, 0.0)
        acc_ref[right] += jnp.where(low, 0.0, tile)


def _add_kernel(count, spans, first, place_ref, ids_ref, slot_ref, got_ref, acc_ref):
    peers = got_ref.shape[0]
    acc_ref[...] = jnp.zeros_like(acc_ref)

    def add_peer(src, carry):
        _scatter(
            got_ref, src, count, peers, spans, first, place_ref, ids_ref, slot_ref, acc_ref
        )
        return carry

    lax.fori_loop(0, peers, add_peer, 0)


def _add_call(count, spans, first, place, ids, slots, got):
    smem = pl.BlockSpec(memory_space=pltpu.SMEM)
    vmem = pl.BlockSpec(memory_space=pltpu.VMEM)
    return pl.pallas_call(
        functools.partial(_add_kernel, count, spans, first),
        in_specs=[smem] * 3 + [vmem],
        out_specs=vmem,
        out_shape=jax.ShapeDtypeStruct((slots.shape[0], got.shape[1], R), F32),
        compiler_params=pltpu.CompilerParams(vmem_limit_bytes=16 << 20),
        cost_estimate=pl.CostEstimate(flops=1000, transcendentals=0, bytes_accessed=1000),
    )(place, ids, slots, got)


def _weight_kernel(count, spans, first, place_ref, ids_ref, slot_ref, got_ref, sum_ref, *refs):
    x_hbm = refs[:-5]
    out_ref, acc_ref, enc_ref, x_refs, sems = refs[-5:]
    peers = got_ref.shape[0]
    blocks, cols = acc_ref.shape[:2]
    owned = blocks // peers
    inner = peers // 2
    upper, lower, sec = place_ref[0], place_ref[1], place_ref[2]
    share = owned // 2
    rows = share * HR

    x_copies = []
    for n in range(len(x_hbm)):
        to = x_refs.at[n // 2, (n % 2) * rows : (n % 2 + 1) * rows, :]
        x_copies.append(pltpu.make_async_copy(x_hbm[n].at[:rows, :], to, sems.at[n]))
    for copy in x_copies:
        copy.start()
    acc_ref[...] = sum_ref[...]

    def add_peer(src, carry):
        _scatter(
            got_ref, src, count, peers, spans, first, place_ref, ids_ref, slot_ref, acc_ref
        )
        return carry

    lax.fori_loop(0, peers, add_peer, 0)
    low = lax.broadcasted_iota(jnp.int32, (cols, R), 1) < HR
    total = None
    for turn in range(inner):
        for far in range(2):
            n = 2 * turn + far
            near_sec = 1 - sec if far else sec
            for side in range(2):
                owner = jnp.bitwise_xor(lower, turn) + inner * (1 - upper if side else upper)
                base = owner * owned + near_sec * share
                for b in range(0, share, 2):
                    even = acc_ref[base + b]
                    odd = acc_ref[base + b + 1]
                    even = even + pltpu.roll(even, HR, 1)
                    odd = odd + pltpu.roll(odd, HR, 1)
                    lo = side * rows + b * HR
                    enc_ref[n, :, lo : lo + 2 * HR] = jnp.where(low, even, odd).astype(BF16)
            x_copies[2 * n].wait()
            x_copies[2 * n + 1].wait()
            part = _dot(enc_ref[n], x_refs[n])
            total = part if total is None else total + part
    scale = (blocks * R) ** (-0.5)
    out_ref[...] = (total * scale).T


def _weight_call(count, spans, first, place, ids, slots, got, partial_sum, xs):
    cols = got.shape[1]
    blocks = slots.shape[0]
    owned = blocks // got.shape[0]
    smem = pl.BlockSpec(memory_space=pltpu.SMEM)
    vmem = pl.BlockSpec(memory_space=pltpu.VMEM)
    xs = [pltpu.with_memory_space_constraint(x, pltpu.HBM) for x in xs]
    pairs = len(xs) // 2
    return pl.pallas_call(
        functools.partial(_weight_kernel, count, spans, first),
        in_specs=[smem] * 3 + [vmem] * 2 + [pl.BlockSpec(memory_space=pl.ANY)] * len(xs),
        out_specs=vmem,
        out_shape=jax.ShapeDtypeStruct((DE, cols), F32),
        scratch_shapes=[
            pltpu.VMEM((blocks, cols, R), F32),
            pltpu.VMEM((pairs, cols, owned * HR), BF16),
            pltpu.VMEM((pairs, owned * HR, DE), BF16),
            pltpu.SemaphoreType.DMA((len(xs),)),
        ],
        compiler_params=pltpu.CompilerParams(vmem_limit_bytes=32 << 20),
        cost_estimate=pl.CostEstimate(
            flops=2 * cols * blocks * HR * DE, transcendentals=0, bytes_accessed=6000000
        ),
    )(place, ids, slots, got, partial_sum, *xs)


def per_device(
    queries,
    grad_out,
    log_sums,
    neighbours,
    key_weight,
    value_weight,
    neighbour_ids,
    block_slot,
    enc_input,
):
    spans = neighbour_ids.shape[0]
    owned = enc_input.shape[0] // R
    peers = lax.axis_size("dp")
    inner = peers // 2
    section = lax.axis_index("section").astype(jnp.int32)
    index = lax.axis_index("dp").astype(jnp.int32)
    upper, lower = index // inner, index % inner
    swap = [(0, 1), (1, 0)]

    held = None
    gots = []
    first = 0
    chunks = (spans // 2, spans - spans // 2)
    for count in chunks:
        held, mine, send = _span_call(
            first,
            count,
            section[None],
            queries,
            grad_out,
            log_sums,
            neighbours,
            key_weight,
            value_weight,
            held,
        )
        if gots:
            mirror, own, send = lax.optimization_barrier((mirror, own, send))
        if not gots:
            enc_input, send = lax.optimization_barrier((enc_input, send))
            id_rows = jnp.pad(neighbour_ids.T.astype(BF16), ((0, 6), (0, DE - spans)))
            split = enc_input.reshape(2, owned // 2, 2, HR, DE)
            split = lax.dynamic_index_in_dim(split, section, 0, keepdims=False)
            own = lax.dynamic_index_in_dim(split, upper, 1, keepdims=False)
            own = jnp.concatenate([own.reshape(owned // 2 * HR, DE), id_rows], axis=0)
            away = lax.dynamic_index_in_dim(split, 1 - upper, 1, keepdims=False)
            away = jnp.concatenate([away.reshape(owned // 2 * HR, DE), id_rows], axis=0)
            mirror = lax.ppermute(away, "dp", [(i, i ^ inner) for i in range(peers)])

            def spread(pack):
                return [pack] + [
                    lax.ppermute(pack, "dp", [(i, i ^ m) for i in range(peers)]) for m in range(1, inner)
                ]

            own = spread(own)
        other = lax.ppermute(send, "section", swap)
        if gots:
            gots[-1], other = lax.optimization_barrier((gots[-1], other))
        ref_grad = (mine.astype(F32) + other.astype(F32)).astype(BF16)
        ref_grad = ref_grad.reshape(peers, DE // peers, count * R)
        if not gots:
            held, ref_grad = lax.optimization_barrier((held, ref_grad))
        gots.append(lax.all_to_all(ref_grad, "dp", 0, 0, tiled=True))
        first += count

    packs = spread(mirror)
    packs = [x for pair in zip(own, packs) for x in pair]
    ids = _ids_call(packs, owned // 2 * HR, id_rows.shape[0])
    ids, packs = lax.optimization_barrier((ids, packs))
    xs = []
    for n in range(0, len(packs), 2):
        xs += packs[n : n + 2] + [lax.ppermute(x, "section", swap) for x in packs[n : n + 2]]
    place = jnp.stack([upper, lower, section])
    ids = pltpu.with_memory_space_constraint(ids, pltpu.HBM)
    partial_sum = _add_call(chunks[0], spans, 0, place, ids, block_slot, gots[0])
    weight = _weight_call(
        chunks[1], spans, chunks[0], place, ids, block_slot, gots[1], partial_sum, xs
    )
    rows = DE // (2 * peers)
    cols = DE // peers
    tiles = lax.all_to_all(weight.reshape(2 * peers, rows, cols), ("dp", "section"), 0, 0, tiled=True)
    tiles = tiles.reshape(2, inner, 2, rows, cols)
    weight_grad = jnp.transpose(tiles[0] + tiles[1], (2, 1, 0, 3)).reshape(rows, DE)
    return (held, weight_grad)


def solution(mesh):
    return jax.shard_map(
        per_device,
        mesh=mesh,
        in_specs=(
            P(("group", "dp"), "section"),
            P(("group", "dp"), "section"),
            P("section", ("group", "dp")),
            P(("group", "dp"), None, None),
            P(None, "section"),
            P(None, "section"),
            P(("group", "dp"), None),
            P("group"),
            P(("group", "dp"), None),
        ),
        out_specs=(P(("group", "dp"), "section"), P(("group", "dp", "section"), None)),
        check_vma=False,
    )
```

```python
import functools

import jax
import jax.numpy as jnp
from jax import lax
from jax.experimental import pallas as pl
from jax.experimental.pallas import tpu as pltpu
from jax.sharding import PartitionSpec as P

HD = 128
DE = 896
CL = 64
R = 128
HR = R // 2
COST = 1 << 36
F32 = jnp.float32
BF16 = jnp.bfloat16
NT = (((1,), (1,)), ((), ()))
TN = (((0,), (0,)), ((), ()))


def _dot(a, b, dims=(((1,), (0,)), ((), ()))):
    return lax.dot_general(a, b, dims, preferred_element_type=F32)


def _span_kernel(first, spans, sec_ref, q_ref, g_ref, l_ref, n_ref, wk_ref, wv_ref, *rest):
    dq_ref, mine_ref, send_ref = rest[-3:]
    sec = sec_ref[0]
    inv_root = HD ** (-0.5)
    pairs = q_ref.shape[1] // (2 * HD)
    rows = []
    for a in range(spans):
        for half in range(2):
            for k in range(2):
                lo = k * R + half * HR
                rows.append(n_ref[a, lo : lo + HR, :])
    rows = jnp.concatenate(rows, axis=0)
    left = lax.broadcasted_iota(jnp.int32, (CL, 2 * HD), 1) < HD
    key_cols = [[] for _ in range(spans)]
    value_cols = [[] for _ in range(spans)]
    for p in range(pairs):
        cols = slice(2 * HD * p, 2 * HD * (p + 1))
        keys = _dot(rows, wk_ref[:, cols]).astype(BF16)
        values = _dot(rows, wv_ref[:, cols]).astype(BF16)
        for a in range(spans):
            ks = keys[2 * R * a : 2 * R * (a + 1)]
            vs = values[2 * R * a : 2 * R * (a + 1)]
            q = q_ref[CL * a : CL * (a + 1), cols]
            g = g_ref[CL * a : CL * (a + 1), cols]
            zero = jnp.zeros_like(q)
            qd = jnp.concatenate([jnp.where(left, q, zero), jnp.where(left, zero, q)], axis=0)
            gd = jnp.concatenate([jnp.where(left, g, zero), jnp.where(left, zero, g)], axis=0)
            at = slice(CL * (first + a), CL * (first + a + 1))
            logs = jnp.concatenate(
                [l_ref[2 * p : 2 * p + 1, at], l_ref[2 * p + 1 : 2 * p + 2, at]], axis=1
            )
            prob = jnp.exp(_dot(ks, qd, NT) * inv_root - logs)
            prob_grad = _dot(vs, gd, NT)
            delta = jnp.sum(prob * prob_grad, axis=0, keepdims=True)
            score_bf = (prob * (prob_grad - delta)).astype(BF16)
            prob_bf = prob.astype(BF16)
            key_cols[a].append((_dot(score_bf, qd) * inv_root).astype(BF16))
            value_cols[a].append(_dot(prob_bf, gd).astype(BF16))
            dq = (_dot(score_bf, ks, TN) * inv_root).astype(BF16)
            dq_ref[CL * a : CL * (a + 1), 2 * HD * p : 2 * HD * p + HD] = dq[:CL, :HD]
            dq_ref[CL * a : CL * (a + 1), 2 * HD * p + HD : 2 * HD * (p + 1)] = dq[CL:, HD:]
    width = DE // 2
    for a in range(spans):
        key_grad = jnp.concatenate(key_cols[a], axis=1)
        value_grad = jnp.concatenate(value_cols[a], axis=1)
        for lane, out_ref in ((sec, mine_ref), (1 - sec, send_ref)):
            at = pl.ds(pl.multiple_of(lane * width, width), width)
            part = _dot(wk_ref[at, :], key_grad, NT) + _dot(wv_ref[at, :], value_grad, NT)
            part = part.astype(BF16)
            for half in range(2):
                out_ref[half, :, R * a : R * (a + 1)] = part[:, half * R : (half + 1) * R]


def _span_call(first, spans, section, queries, grad_out, log_sums, neighbours, kw, vw, held):
    tokens, columns = queries.shape
    heads = log_sums.shape[0]
    whole = lambda i, s: (0, 0)
    block = first // spans
    in_specs = [
        pl.BlockSpec((spans * CL, columns), lambda i, s: (block, 0)),
        pl.BlockSpec((spans * CL, columns), lambda i, s: (block, 0)),
        pl.BlockSpec((heads, tokens), whole),
        pl.BlockSpec((spans, 2 * R, DE), lambda i, s: (block, 0, 0)),
        pl.BlockSpec((DE, columns), whole),
        pl.BlockSpec((DE, columns), whole),
    ]
    args = [queries, grad_out, log_sums, neighbours, kw, vw]
    args = [pltpu.with_memory_space_constraint(x, pltpu.HBM) for x in args]
    aliases = {}
    if held is not None:
        in_specs.append(pl.BlockSpec(memory_space=pl.ANY))
        args.append(held)
        aliases = {len(args): 0}
    half_spec = pl.BlockSpec((2, DE // 2, spans * R), lambda i, s: (0, 0, 0))
    half_shape = jax.ShapeDtypeStruct((2, DE // 2, spans * R), BF16)
    return pl.pallas_call(
        functools.partial(_span_kernel, first, spans),
        grid_spec=pltpu.PrefetchScalarGridSpec(
            num_scalar_prefetch=1,
            grid=(1,),
            in_specs=in_specs,
            out_specs=[
                pl.BlockSpec((spans * CL, columns), lambda i, s: (block, 0)),
                half_spec,
                half_spec,
            ],
        ),
        out_shape=[jax.ShapeDtypeStruct((tokens, columns), BF16), half_shape, half_shape],
        input_output_aliases=aliases,
        compiler_params=pltpu.CompilerParams(vmem_limit_bytes=48 << 20),
        cost_estimate=pl.CostEstimate(
            flops=spans * 2 * R * columns * (8 * DE + 10 * CL),
            transcendentals=spans * 2 * R * CL * heads,
            bytes_accessed=4 * DE * columns + spans * 1000000,
        ),
    )(section, *args)


def _ids_kernel(*refs):
    out_ref = refs[-1]
    for n, x_ref in enumerate(refs[:-1]):
        table = x_ref[...].astype(F32).astype(jnp.int32)
        out_ref[2 * n : 2 * n + 2, :] = table[:2, :]


def _ids_call(packs, start, rows):
    spec = pl.BlockSpec((rows, R), lambda i: (start // rows, 0))
    return pl.pallas_call(
        _ids_kernel,
        grid=(1,),
        in_specs=[spec] * len(packs),
        out_specs=pl.BlockSpec((2 * len(packs), R), lambda i: (0, 0)),
        out_shape=jax.ShapeDtypeStruct((2 * len(packs), R), jnp.int32),
        cost_estimate=pl.CostEstimate(flops=COST, transcendentals=0, bytes_accessed=1000),
    )(*packs)


def _scatter(got, src, count, peers, spans, first, place_ref, ids_ref, slot_ref, acc_ref):
    inner = peers // 2
    low = lax.broadcasted_iota(jnp.int32, acc_ref.shape[1:], 1) < HR
    turn = jnp.bitwise_xor(src % inner, place_ref[1])
    side = jnp.bitwise_xor(src // inner, place_ref[0])
    at = (2 * turn + side) * 2
    for c in range(count):
        tile = got[src, :, R * c : R * (c + 1)].astype(F32)
        left = slot_ref[ids_ref[at, first + c]]
        right = slot_ref[ids_ref[at + 1, first + c]]
        acc_ref[left] += jnp.where(low, tile, 0.0)
        acc_ref[right] += jnp.where(low, 0.0, tile)


def _add_kernel(count, spans, first, place_ref, ids_ref, slot_ref, got_ref, acc_ref):
    peers = got_ref.shape[0]
    acc_ref[...] = jnp.zeros_like(acc_ref)

    def add_peer(src, carry):
        _scatter(
            got_ref, src, count, peers, spans, first, place_ref, ids_ref, slot_ref, acc_ref
        )
        return carry

    lax.fori_loop(0, peers, add_peer, 0)


def _add_call(count, spans, first, place, ids, slots, got):
    smem = pl.BlockSpec(memory_space=pltpu.SMEM)
    vmem = pl.BlockSpec(memory_space=pltpu.VMEM)
    return pl.pallas_call(
        functools.partial(_add_kernel, count, spans, first),
        in_specs=[smem] * 3 + [vmem],
        out_specs=vmem,
        out_shape=jax.ShapeDtypeStruct((slots.shape[0], got.shape[1], R), F32),
        compiler_params=pltpu.CompilerParams(vmem_limit_bytes=16 << 20),
        cost_estimate=pl.CostEstimate(flops=1000, transcendentals=0, bytes_accessed=1000),
    )(place, ids, slots, got)


def _weight_kernel(count, spans, first, place_ref, ids_ref, slot_ref, got_ref, sum_ref, *refs):
    x_hbm = refs[:-5]
    out_ref, acc_ref, enc_ref, x_refs, sems = refs[-5:]
    peers = got_ref.shape[0]
    blocks, cols = acc_ref.shape[:2]
    owned = blocks // peers
    inner = peers // 2
    upper, lower, sec = place_ref[0], place_ref[1], place_ref[2]
    share = owned // 2
    rows = share * HR

    x_copies = []
    for n in range(len(x_hbm)):
        to = x_refs.at[n // 2, (n % 2) * rows : (n % 2 + 1) * rows, :]
        x_copies.append(pltpu.make_async_copy(x_hbm[n].at[:rows, :], to, sems.at[n]))
    for copy in x_copies:
        copy.start()
    acc_ref[...] = sum_ref[...]

    def add_peer(src, carry):
        _scatter(
            got_ref, src, count, peers, spans, first, place_ref, ids_ref, slot_ref, acc_ref
        )
        return carry

    lax.fori_loop(0, peers, add_peer, 0)
    low = lax.broadcasted_iota(jnp.int32, (cols, R), 1) < HR
    total = None
    for turn in range(inner):
        for far in range(2):
            n = 2 * turn + far
            near_sec = 1 - sec if far else sec
            for side in range(2):
                owner = jnp.bitwise_xor(lower, turn) + inner * (1 - upper if side else upper)
                base = owner * owned + near_sec * share
                for b in range(0, share, 2):
                    even = acc_ref[base + b]
                    odd = acc_ref[base + b + 1]
                    even = even + pltpu.roll(even, HR, 1)
                    odd = odd + pltpu.roll(odd, HR, 1)
                    lo = side * rows + b * HR
                    enc_ref[n, :, lo : lo + 2 * HR] = jnp.where(low, even, odd).astype(BF16)
            x_copies[2 * n].wait()
            x_copies[2 * n + 1].wait()
            part = _dot(enc_ref[n], x_refs[n])
            total = part if total is None else total + part
    scale = (blocks * R) ** (-0.5)
    out_ref[...] = (total * scale).T


def _weight_call(count, spans, first, place, ids, slots, got, partial_sum, xs):
    cols = got.shape[1]
    blocks = slots.shape[0]
    owned = blocks // got.shape[0]
    smem = pl.BlockSpec(memory_space=pltpu.SMEM)
    vmem = pl.BlockSpec(memory_space=pltpu.VMEM)
    xs = [pltpu.with_memory_space_constraint(x, pltpu.HBM) for x in xs]
    pairs = len(xs) // 2
    return pl.pallas_call(
        functools.partial(_weight_kernel, count, spans, first),
        in_specs=[smem] * 3 + [vmem] * 2 + [pl.BlockSpec(memory_space=pl.ANY)] * len(xs),
        out_specs=vmem,
        out_shape=jax.ShapeDtypeStruct((DE, cols), F32),
        scratch_shapes=[
            pltpu.VMEM((blocks, cols, R), F32),
            pltpu.VMEM((pairs, cols, owned * HR), BF16),
            pltpu.VMEM((pairs, owned * HR, DE), BF16),
            pltpu.SemaphoreType.DMA((len(xs),)),
        ],
        compiler_params=pltpu.CompilerParams(vmem_limit_bytes=32 << 20),
        cost_estimate=pl.CostEstimate(
            flops=2 * cols * blocks * HR * DE, transcendentals=0, bytes_accessed=6000000
        ),
    )(place, ids, slots, got, partial_sum, *xs)


def per_device(
    queries,
    grad_out,
    log_sums,
    neighbours,
    key_weight,
    value_weight,
    neighbour_ids,
    block_slot,
    enc_input,
):
    spans = neighbour_ids.shape[0]
    owned = enc_input.shape[0] // R
    peers = lax.axis_size("dp")
    inner = peers // 2
    section = lax.axis_index("section").astype(jnp.int32)
    index = lax.axis_index("dp").astype(jnp.int32)
    upper, lower = index // inner, index % inner
    swap = [(0, 1), (1, 0)]

    held = None
    gots = []
    first = 0
    chunks = (spans // 2, spans - spans // 2)
    for count in chunks:
        held, mine, send = _span_call(
            first,
            count,
            section[None],
            queries,
            grad_out,
            log_sums,
            neighbours,
            key_weight,
            value_weight,
            held,
        )
        if gots:
            mirror, own, send = lax.optimization_barrier((mirror, own, send))
        if not gots:
            enc_input, send = lax.optimization_barrier((enc_input, send))
            id_rows = jnp.pad(neighbour_ids.T.astype(BF16), ((0, 6), (0, DE - spans)))
            split = enc_input.reshape(2, owned // 2, 2, HR, DE)
            split = lax.dynamic_index_in_dim(split, section, 0, keepdims=False)
            own = lax.dynamic_index_in_dim(split, upper, 1, keepdims=False)
            own = jnp.concatenate([own.reshape(owned // 2 * HR, DE), id_rows], axis=0)
            away = lax.dynamic_index_in_dim(split, 1 - upper, 1, keepdims=False)
            away = jnp.concatenate([away.reshape(owned // 2 * HR, DE), id_rows], axis=0)
            mirror = lax.ppermute(away, "dp", [(i, i ^ inner) for i in range(peers)])

            def spread(pack):
                return [pack] + [
                    lax.ppermute(pack, "dp", [(i, i ^ m) for i in range(peers)]) for m in range(1, inner)
                ]

            own = spread(own)
        other = lax.ppermute(send, "section", swap)
        if gots:
            gots[-1], other = lax.optimization_barrier((gots[-1], other))
        ref_grad = (mine.astype(F32) + other.astype(F32)).astype(BF16)
        ref_grad = ref_grad.reshape(peers, DE // peers, count * R)
        if not gots:
            held, ref_grad = lax.optimization_barrier((held, ref_grad))
        gots.append(lax.all_to_all(ref_grad, "dp", 0, 0, tiled=True))
        first += count

    packs = spread(mirror)
    packs = [x for pair in zip(own, packs) for x in pair]
    ids = _ids_call(packs, owned // 2 * HR, id_rows.shape[0])
    ids, far = lax.optimization_barrier((ids, packs[1::2]))
    xs = []
    for near, x in zip(packs[::2], far):
        xs += [near, x] + [lax.ppermute(y, "section", swap) for y in (near, x)]
    place = jnp.stack([upper, lower, section])
    ids = pltpu.with_memory_space_constraint(ids, pltpu.HBM)
    partial_sum = _add_call(chunks[0], spans, 0, place, ids, block_slot, gots[0])
    weight = _weight_call(
        chunks[1], spans, chunks[0], place, ids, block_slot, gots[1], partial_sum, xs
    )
    rows = DE // (2 * peers)
    cols = DE // peers
    tiles = lax.all_to_all(weight.reshape(2 * peers, rows, cols), ("dp", "section"), 0, 0, tiled=True)
    tiles = tiles.reshape(2, inner, 2, rows, cols)
    weight_grad = jnp.transpose(tiles[0] + tiles[1], (2, 1, 0, 3)).reshape(rows, DE)
    return (held, weight_grad)


def solution(mesh):
    return jax.shard_map(
        per_device,
        mesh=mesh,
        in_specs=(
            P(("group", "dp"), "section"),
            P(("group", "dp"), "section"),
            P("section", ("group", "dp")),
            P(("group", "dp"), None, None),
            P(None, "section"),
            P(None, "section"),
            P(("group", "dp"), None),
            P("group"),
            P(("group", "dp"), None),
        ),
        out_specs=(P(("group", "dp"), "section"), P(("group", "dp", "section"), None)),
        check_vma=False,
    )
```

```python
import functools

import jax
import jax.numpy as jnp
from jax import lax
from jax.experimental import pallas as pl
from jax.experimental.pallas import tpu as pltpu
from jax.sharding import PartitionSpec as P

HD = 128
DE = 896
CL = 64
R = 128
HR = R // 2
COST = 1 << 36
F32 = jnp.float32
BF16 = jnp.bfloat16
NT = (((1,), (1,)), ((), ()))
TN = (((0,), (0,)), ((), ()))


def _dot(a, b, dims=(((1,), (0,)), ((), ()))):
    return lax.dot_general(a, b, dims, preferred_element_type=F32)


def _span_kernel(first, spans, sec_ref, q_ref, g_ref, l_ref, n_ref, wk_ref, wv_ref, *rest):
    dq_ref, mine_ref, send_ref = rest[-3:]
    sec = sec_ref[0]
    inv_root = HD ** (-0.5)
    pairs = q_ref.shape[1] // (2 * HD)
    rows = []
    for a in range(spans):
        for half in range(2):
            for k in range(2):
                lo = k * R + half * HR
                rows.append(n_ref[a, lo : lo + HR, :])
    rows = jnp.concatenate(rows, axis=0)
    left = lax.broadcasted_iota(jnp.int32, (CL, 2 * HD), 1) < HD
    key_cols = [[] for _ in range(spans)]
    value_cols = [[] for _ in range(spans)]
    for p in range(pairs):
        cols = slice(2 * HD * p, 2 * HD * (p + 1))
        keys = _dot(rows, wk_ref[:, cols]).astype(BF16)
        values = _dot(rows, wv_ref[:, cols]).astype(BF16)
        for a in range(spans):
            ks = keys[2 * R * a : 2 * R * (a + 1)]
            vs = values[2 * R * a : 2 * R * (a + 1)]
            q = q_ref[CL * a : CL * (a + 1), cols]
            g = g_ref[CL * a : CL * (a + 1), cols]
            zero = jnp.zeros_like(q)
            qd = jnp.concatenate([jnp.where(left, q, zero), jnp.where(left, zero, q)], axis=0)
            gd = jnp.concatenate([jnp.where(left, g, zero), jnp.where(left, zero, g)], axis=0)
            at = slice(CL * (first + a), CL * (first + a + 1))
            logs = jnp.concatenate(
                [l_ref[2 * p : 2 * p + 1, at], l_ref[2 * p + 1 : 2 * p + 2, at]], axis=1
            )
            prob = jnp.exp(_dot(ks, qd, NT) * inv_root - logs)
            prob_grad = _dot(vs, gd, NT)
            delta = jnp.sum(prob * prob_grad, axis=0, keepdims=True)
            score_bf = (prob * (prob_grad - delta)).astype(BF16)
            prob_bf = prob.astype(BF16)
            key_cols[a].append((_dot(score_bf, qd) * inv_root).astype(BF16))
            value_cols[a].append(_dot(prob_bf, gd).astype(BF16))
            dq = (_dot(score_bf, ks, TN) * inv_root).astype(BF16)
            dq_ref[CL * a : CL * (a + 1), 2 * HD * p : 2 * HD * p + HD] = dq[:CL, :HD]
            dq_ref[CL * a : CL * (a + 1), 2 * HD * p + HD : 2 * HD * (p + 1)] = dq[CL:, HD:]
    width = DE // 2
    for a in range(spans):
        key_grad = jnp.concatenate(key_cols[a], axis=1)
        value_grad = jnp.concatenate(value_cols[a], axis=1)
        for lane, out_ref in ((sec, mine_ref), (1 - sec, send_ref)):
            at = pl.ds(pl.multiple_of(lane * width, width), width)
            part = _dot(wk_ref[at, :], key_grad, NT) + _dot(wv_ref[at, :], value_grad, NT)
            part = part.astype(BF16)
            for half in range(2):
                out_ref[half, :, R * a : R * (a + 1)] = part[:, half * R : (half + 1) * R]


def _span_call(first, spans, section, queries, grad_out, log_sums, neighbours, kw, vw, held):
    tokens, columns = queries.shape
    heads = log_sums.shape[0]
    whole = lambda i, s: (0, 0)
    block = first // spans
    in_specs = [
        pl.BlockSpec((spans * CL, columns), lambda i, s: (block, 0)),
        pl.BlockSpec((spans * CL, columns), lambda i, s: (block, 0)),
        pl.BlockSpec((heads, tokens), whole),
        pl.BlockSpec((spans, 2 * R, DE), lambda i, s: (block, 0, 0)),
        pl.BlockSpec((DE, columns), whole),
        pl.BlockSpec((DE, columns), whole),
    ]
    args = [queries, grad_out, log_sums, neighbours, kw, vw]
    args = [pltpu.with_memory_space_constraint(x, pltpu.HBM) for x in args]
    aliases = {}
    if held is not None:
        in_specs.append(pl.BlockSpec(memory_space=pl.ANY))
        args.append(held)
        aliases = {len(args): 0}
    half_spec = pl.BlockSpec((2, DE // 2, spans * R), lambda i, s: (0, 0, 0))
    half_shape = jax.ShapeDtypeStruct((2, DE // 2, spans * R), BF16)
    return pl.pallas_call(
        functools.partial(_span_kernel, first, spans),
        grid_spec=pltpu.PrefetchScalarGridSpec(
            num_scalar_prefetch=1,
            grid=(1,),
            in_specs=in_specs,
            out_specs=[
                pl.BlockSpec((spans * CL, columns), lambda i, s: (block, 0)),
                half_spec,
                half_spec,
            ],
        ),
        out_shape=[jax.ShapeDtypeStruct((tokens, columns), BF16), half_shape, half_shape],
        input_output_aliases=aliases,
        compiler_params=pltpu.CompilerParams(vmem_limit_bytes=48 << 20),
        cost_estimate=pl.CostEstimate(
            flops=spans * 2 * R * columns * (8 * DE + 10 * CL),
            transcendentals=spans * 2 * R * CL * heads,
            bytes_accessed=4 * DE * columns + spans * 1000000,
        ),
    )(section, *args)


def _ids_kernel(*refs):
    out_ref = refs[-1]
    for n, x_ref in enumerate(refs[:-1]):
        table = x_ref[...].astype(F32).astype(jnp.int32)
        out_ref[2 * n : 2 * n + 2, :] = table[:2, :]


def _ids_call(packs, start, rows):
    spec = pl.BlockSpec((rows, R), lambda i: (start // rows, 0))
    return pl.pallas_call(
        _ids_kernel,
        grid=(1,),
        in_specs=[spec] * len(packs),
        out_specs=pl.BlockSpec((2 * len(packs), R), lambda i: (0, 0)),
        out_shape=jax.ShapeDtypeStruct((2 * len(packs), R), jnp.int32),
        cost_estimate=pl.CostEstimate(flops=COST, transcendentals=0, bytes_accessed=1000),
    )(*packs)


def _scatter(got, src, count, peers, spans, first, place_ref, ids_ref, slot_ref, acc_ref):
    inner = peers // 2
    low = lax.broadcasted_iota(jnp.int32, acc_ref.shape[1:], 1) < HR
    turn = jnp.bitwise_xor(src % inner, place_ref[1])
    side = jnp.bitwise_xor(src // inner, place_ref[0])
    at = (2 * turn + side) * 2
    for c in range(count):
        tile = got[src, :, R * c : R * (c + 1)].astype(F32)
        left = slot_ref[ids_ref[at, first + c]]
        right = slot_ref[ids_ref[at + 1, first + c]]
        acc_ref[left] += jnp.where(low, tile, 0.0)
        acc_ref[right] += jnp.where(low, 0.0, tile)


def _add_kernel(count, spans, first, place_ref, ids_ref, slot_ref, got_ref, acc_ref):
    peers = got_ref.shape[0]
    acc_ref[...] = jnp.zeros_like(acc_ref)

    def add_peer(src, carry):
        _scatter(
            got_ref, src, count, peers, spans, first, place_ref, ids_ref, slot_ref, acc_ref
        )
        return carry

    lax.fori_loop(0, peers, add_peer, 0)


def _add_call(count, spans, first, place, ids, slots, got):
    smem = pl.BlockSpec(memory_space=pltpu.SMEM)
    vmem = pl.BlockSpec(memory_space=pltpu.VMEM)
    return pl.pallas_call(
        functools.partial(_add_kernel, count, spans, first),
        in_specs=[smem] * 3 + [vmem],
        out_specs=vmem,
        out_shape=jax.ShapeDtypeStruct((slots.shape[0], got.shape[1], R), F32),
        compiler_params=pltpu.CompilerParams(vmem_limit_bytes=16 << 20),
        cost_estimate=pl.CostEstimate(flops=1000, transcendentals=0, bytes_accessed=1000),
    )(place, ids, slots, got)


def _weight_kernel(count, spans, first, place_ref, ids_ref, slot_ref, got_ref, sum_ref, *refs):
    x_hbm = refs[:-5]
    out_ref, acc_ref, enc_ref, x_refs, sems = refs[-5:]
    peers = got_ref.shape[0]
    blocks, cols = acc_ref.shape[:2]
    owned = blocks // peers
    inner = peers // 2
    upper, lower, sec = place_ref[0], place_ref[1], place_ref[2]
    share = owned // 2
    rows = share * HR

    x_copies = []
    for n in range(len(x_hbm)):
        to = x_refs.at[n * rows : (n + 1) * rows, :]
        x_copies.append(pltpu.make_async_copy(x_hbm[n].at[:rows, :], to, sems.at[n]))
    for copy in x_copies:
        copy.start()
    acc_ref[...] = sum_ref[...]

    def add_peer(src, carry):
        _scatter(
            got_ref, src, count, peers, spans, first, place_ref, ids_ref, slot_ref, acc_ref
        )
        return carry

    lax.fori_loop(0, peers, add_peer, 0)
    low = lax.broadcasted_iota(jnp.int32, (cols, R), 1) < HR
    for turn in range(inner):
        for far in range(2):
            n = 2 * turn + far
            near_sec = 1 - sec if far else sec
            for side in range(2):
                owner = jnp.bitwise_xor(lower, turn) + inner * (1 - upper if side else upper)
                base = owner * owned + near_sec * share
                for b in range(0, share, 2):
                    even = acc_ref[base + b]
                    odd = acc_ref[base + b + 1]
                    even = even + pltpu.roll(even, HR, 1)
                    odd = odd + pltpu.roll(odd, HR, 1)
                    lo = (2 * n + side) * rows + b * HR
                    enc_ref[:, lo : lo + 2 * HR] = jnp.where(low, even, odd).astype(BF16)
    for copy in x_copies:
        copy.wait()
    total = _dot(enc_ref[...], x_refs[...])
    scale = (blocks * R) ** (-0.5)
    out_ref[...] = (total * scale).T


def _weight_call(count, spans, first, place, ids, slots, got, partial_sum, xs):
    cols = got.shape[1]
    blocks = slots.shape[0]
    owned = blocks // got.shape[0]
    smem = pl.BlockSpec(memory_space=pltpu.SMEM)
    vmem = pl.BlockSpec(memory_space=pltpu.VMEM)
    xs = [pltpu.with_memory_space_constraint(x, pltpu.HBM) for x in xs]
    return pl.pallas_call(
        functools.partial(_weight_kernel, count, spans, first),
        in_specs=[smem] * 3 + [vmem] * 2 + [pl.BlockSpec(memory_space=pl.ANY)] * len(xs),
        out_specs=vmem,
        out_shape=jax.ShapeDtypeStruct((DE, cols), F32),
        scratch_shapes=[
            pltpu.VMEM((blocks, cols, R), F32),
            pltpu.VMEM((cols, blocks * HR), BF16),
            pltpu.VMEM((blocks * HR, DE), BF16),
            pltpu.SemaphoreType.DMA((len(xs),)),
        ],
        compiler_params=pltpu.CompilerParams(vmem_limit_bytes=32 << 20),
        cost_estimate=pl.CostEstimate(
            flops=2 * cols * blocks * HR * DE, transcendentals=0, bytes_accessed=6000000
        ),
    )(place, ids, slots, got, partial_sum, *xs)


def per_device(
    queries,
    grad_out,
    log_sums,
    neighbours,
    key_weight,
    value_weight,
    neighbour_ids,
    block_slot,
    enc_input,
):
    spans = neighbour_ids.shape[0]
    owned = enc_input.shape[0] // R
    peers = lax.axis_size("dp")
    inner = peers // 2
    section = lax.axis_index("section").astype(jnp.int32)
    index = lax.axis_index("dp").astype(jnp.int32)
    upper, lower = index // inner, index % inner
    swap = [(0, 1), (1, 0)]

    held = None
    gots = []
    first = 0
    chunks = (spans // 2, spans - spans // 2)
    for count in chunks:
        held, mine, send = _span_call(
            first,
            count,
            section[None],
            queries,
            grad_out,
            log_sums,
            neighbours,
            key_weight,
            value_weight,
            held,
        )
        if gots:
            mirror, own, send = lax.optimization_barrier((mirror, own, send))
        if not gots:
            enc_input, send = lax.optimization_barrier((enc_input, send))
            id_rows = jnp.pad(neighbour_ids.T.astype(BF16), ((0, 6), (0, DE - spans)))
            split = enc_input.reshape(2, owned // 2, 2, HR, DE)
            split = lax.dynamic_index_in_dim(split, section, 0, keepdims=False)
            own = lax.dynamic_index_in_dim(split, upper, 1, keepdims=False)
            own = jnp.concatenate([own.reshape(owned // 2 * HR, DE), id_rows], axis=0)
            away = lax.dynamic_index_in_dim(split, 1 - upper, 1, keepdims=False)
            away = jnp.concatenate([away.reshape(owned // 2 * HR, DE), id_rows], axis=0)
            mirror = lax.ppermute(away, "dp", [(i, i ^ inner) for i in range(peers)])

            def spread(pack):
                return [pack] + [
                    lax.ppermute(pack, "dp", [(i, i ^ m) for i in range(peers)]) for m in range(1, inner)
                ]

            own = spread(own)
        other = lax.ppermute(send, "section", swap)
        if gots:
            gots[-1], other = lax.optimization_barrier((gots[-1], other))
        ref_grad = (mine.astype(F32) + other.astype(F32)).astype(BF16)
        ref_grad = ref_grad.reshape(peers, DE // peers, count * R)
        if not gots:
            held, ref_grad = lax.optimization_barrier((held, ref_grad))
        gots.append(lax.all_to_all(ref_grad, "dp", 0, 0, tiled=True))
        first += count

    packs = spread(mirror)
    packs = [x for pair in zip(own, packs) for x in pair]
    ids = _ids_call(packs, owned // 2 * HR, id_rows.shape[0])
    ids, packs = lax.optimization_barrier((ids, packs))
    xs = []
    for n in range(0, len(packs), 2):
        xs += packs[n : n + 2] + [lax.ppermute(x, "section", swap) for x in packs[n : n + 2]]
    place = jnp.stack([upper, lower, section])
    ids = pltpu.with_memory_space_constraint(ids, pltpu.HBM)
    partial_sum = _add_call(chunks[0], spans, 0, place, ids, block_slot, gots[0])
    weight = _weight_call(
        chunks[1], spans, chunks[0], place, ids, block_slot, gots[1], partial_sum, xs
    )
    rows = DE // (2 * peers)
    cols = DE // peers
    tiles = lax.all_to_all(weight.reshape(2 * peers, rows, cols), ("dp", "section"), 0, 0, tiled=True)
    tiles = tiles.reshape(2, inner, 2, rows, cols)
    weight_grad = jnp.transpose(tiles[0] + tiles[1], (2, 1, 0, 3)).reshape(rows, DE)
    return (held, weight_grad)


def solution(mesh):
    return jax.shard_map(
        per_device,
        mesh=mesh,
        in_specs=(
            P(("group", "dp"), "section"),
            P(("group", "dp"), "section"),
            P("section", ("group", "dp")),
            P(("group", "dp"), None, None),
            P(None, "section"),
            P(None, "section"),
            P(("group", "dp"), None),
            P("group"),
            P(("group", "dp"), None),
        ),
        out_specs=(P(("group", "dp"), "section"), P(("group", "dp", "section"), None)),
        check_vma=False,
    )
```
